256 devices in a mesh: seq: 64 (over z, x, y_lo), sub: 4 (over y_hi, core).
Axes of the slice: x: 4, y: 4 (y_hi: 2, y_lo: 2; y = y_hi * 2 + y_lo), z: 8, core: 2. Of those that a mesh axis runs over, the one named last changes fastest.
Arguments:
- features: bfloat16 [262144, 768], P(('seq', 'sub')), may hold values from -6 to 6
- kernel: bfloat16 [3, 768, 384], replicated, may hold values from -0.125 to 0.125
- offsets: float32 [384], replicated, may hold values from -3 to 3
- mixer: bfloat16 [384, 768], replicated, may hold values from -0.3125 to 0.3125
- biases: float32 [768], replicated, may hold values from -3 to 3
- cotangent: bfloat16 [262144, 768], P(('seq', 'sub')), may hold values from -6 to 6
Outputs:
- layer_output: bfloat16 [262144, 768], P(('seq', 'sub'))
- input_grad: bfloat16 [262144, 768], P(('seq', 'sub'))
- kernel_grad: float32 [3, 768, 384], replicated
- offset_grad: float32 [384], replicated
- mixer_grad: float32 [384, 768], replicated
- biases_grad: float32 [768], replicated
The draws below stay inside these ranges and needn't reach their ends.
All inputs are finite; a program needn't handle non-finite values.
Results may differ from the reference program's by a relative error of at most 0.0075.
Values may be sent and summed in bfloat16 or wider, within the bound.
A program may use at most 64 MiB of HBM per device.

```python
import math
import jax
import jax.numpy as jnp
from jax import lax

C = 768
H = 384
DILATION_STEP = 8192
LENGTH = 262144


def block_scale(rng, dims, split, smallest, high):
    level, own = 1.0, jax.random.fold_in(rng, 6)
    for axis_at, parts in split:
        heights = jnp.exp(jax.random.uniform(jax.random.fold_in(own, axis_at), (parts,), jnp.float32, smallest / len(split), high / len(split)))
        level = level * jnp.repeat(heights, dims[axis_at] // parts).reshape([-1 if axis == axis_at else 1 for axis in range(len(dims))])
    return level


def noise(own_key, shape, scale, most, pieces=(), held_as=jnp.bfloat16):
    gain = block_scale(own_key, shape, pieces, -0.22, 0.18) if pieces else 1.0
    drawn = jax.random.normal(own_key, shape, jnp.float32) * scale * gain
    return jnp.minimum(jnp.maximum(drawn, -most), most).astype(held_as)


def setup_inputs(seed: int = 0) -> dict:
    key_list = jax.random.split(jax.random.key(seed), 7)
    return {
        "features": noise(key_list[0], (LENGTH, C), 1.0, 6.0, ((0, 256),)),
        "kernel": noise(key_list[1], (3, C, H), (3 * C) ** -0.5, 0.125),
        "offsets": noise(key_list[2], (H,), 0.5, 3.0, (), jnp.float32),
        "mixer": noise(key_list[3], (H, C), H ** -0.5, 0.3125),
        "biases": noise(key_list[4], (C,), 0.5, 3.0, (), jnp.float32),
        "cotangent": noise(key_list[5], (LENGTH, C), 1.0, 6.0, ((0, 256),)),
    }


def gelu_exact(values):
    return jax.nn.gelu(values, approximate=False)

def gelu_slope(values):
    normal_cdf = 0.5 * (1.0 + jax.scipy.special.erf(values / math.sqrt(2.0)))
    return normal_cdf + values * jnp.exp(-0.5 * values * values) / math.sqrt(2.0 * math.pi)

def contract_rows(left, right):
    return jnp.dot(left.T, right, preferred_element_type=jnp.float32)

def reference(features, kernel, offsets, mixer, biases, cotangent):
    inputs = features.astype(jnp.float32)
    activated_output = gelu_exact(inputs).astype(jnp.bfloat16)
    behind_neighbor = jnp.roll(activated_output, DILATION_STEP, axis=0)
    ahead_neighbor = jnp.roll(activated_output, -DILATION_STEP, axis=0)
    tap_early = jnp.dot(behind_neighbor, kernel[0], preferred_element_type=jnp.float32).astype(jnp.bfloat16)
    tap_late = jnp.dot(ahead_neighbor, kernel[2], preferred_element_type=jnp.float32).astype(jnp.bfloat16)
    preact = jnp.dot(activated_output, kernel[1], preferred_element_type=jnp.float32) + tap_early.astype(jnp.float32) + tap_late.astype(jnp.float32) + offsets
    hidden = gelu_exact(preact).astype(jnp.bfloat16)
    layer_output = (inputs + jnp.dot(hidden, mixer, preferred_element_type=jnp.float32) + biases).astype(jnp.bfloat16)
    factor = 1.0 / math.sqrt(LENGTH)
    cot_float = cotangent.astype(jnp.float32)
    mixer_grad = contract_rows(hidden, cotangent) * factor
    biases_grad = lax.optimization_barrier(jnp.sum(cot_float, axis=0)) * factor
    hidden_grad = jnp.dot(cotangent, mixer.T, preferred_element_type=jnp.float32)
    preactivation_grad = (hidden_grad * gelu_slope(preact)).astype(jnp.bfloat16)
    kernel_grad = jnp.stack([contract_rows(behind_neighbor, preactivation_grad), contract_rows(activated_output, preactivation_grad), contract_rows(ahead_neighbor, preactivation_grad)]) * factor
    offset_grad = lax.optimization_barrier(jnp.sum(preactivation_grad.astype(jnp.float32), axis=0)) * factor
    activated_output_grad = jnp.dot(jnp.roll(preactivation_grad, -DILATION_STEP, axis=0), kernel[0].T, preferred_element_type=jnp.float32) + jnp.dot(preactivation_grad, kernel[1].T, preferred_element_type=jnp.float32) + jnp.dot(jnp.roll(preactivation_grad, DILATION_STEP, axis=0), kernel[2].T, preferred_element_type=jnp.float32)
    input_grad = (cot_float + activated_output_grad * gelu_slope(inputs)).astype(jnp.bfloat16)
    return (layer_output, input_grad, kernel_grad, offset_grad, mixer_grad, biases_grad)
```

```python
import math

import jax
import jax.numpy as jnp
from jax import lax
from jax.sharding import PartitionSpec as P

DILATION_STEP = 8192


def from_behind(value, axis, steps):
    count = lax.axis_size(axis)
    pairs = [(source, (source + steps) % count) for source in range(count)]
    return lax.ppermute(value, axis, pairs)


def gelu_exact(values):
    return jax.nn.gelu(values, approximate=False)


def gelu_slope(values):
    normal_cdf = 0.5 * (1.0 + jax.scipy.special.erf(values / math.sqrt(2.0)))
    return normal_cdf + values * jnp.exp(-0.5 * values * values) / math.sqrt(2.0 * math.pi)


def contract_rows(left, right):
    return lax.dot_general(
        left, right, (((0,), (0,)), ((), ())), preferred_element_type=jnp.float32
    )


def times_transposed(left, right):
    return lax.dot_general(
        left, right, (((1,), (1,)), ((), ())), preferred_element_type=jnp.float32
    )


def local(features, kernel, offsets, mixer, biases, cotangent):
    partition_rows = features.shape[0]
    offset_distance = DILATION_STEP // (partition_rows * lax.axis_size("sub"))
    factor = 1.0 / math.sqrt(partition_rows * lax.axis_size("seq") * lax.axis_size("sub"))
    inputs = features.astype(jnp.float32)
    activated_output = gelu_exact(inputs).astype(jnp.bfloat16)
    send_early = jnp.dot(activated_output, kernel[0], preferred_element_type=jnp.float32).astype(
        jnp.bfloat16
    )
    send_late = jnp.dot(activated_output, kernel[2], preferred_element_type=jnp.float32).astype(
        jnp.bfloat16
    )
    tap_early = from_behind(send_early, "seq", offset_distance)
    tap_late = from_behind(send_late, "seq", -offset_distance)
    preact = (
        jnp.dot(activated_output, kernel[1], preferred_element_type=jnp.float32)
        + tap_early.astype(jnp.float32)
        + tap_late.astype(jnp.float32)
        + offsets
    )
    hidden = gelu_exact(preact).astype(jnp.bfloat16)
    layer_output = (
        inputs + jnp.dot(hidden, mixer, preferred_element_type=jnp.float32) + biases
    ).astype(jnp.bfloat16)
    cot_float = cotangent.astype(jnp.float32)
    mixer_part = contract_rows(hidden, cotangent) * factor
    biases_part = jnp.sum(cot_float, axis=0) * factor
    hidden_grad = times_transposed(cotangent, mixer)
    preactivation_grad = (hidden_grad * gelu_slope(preact)).astype(jnp.bfloat16)
    grad_later = from_behind(preactivation_grad, "seq", -offset_distance)
    grad_earlier = from_behind(preactivation_grad, "seq", offset_distance)
    kernel_part = (
        jnp.stack(
            [
                contract_rows(activated_output, grad_later),
                contract_rows(activated_output, preactivation_grad),
                contract_rows(activated_output, grad_earlier),
            ]
        )
        * factor
    )
    offset_part = jnp.sum(preactivation_grad.astype(jnp.float32), axis=0) * factor
    activated_output_grad = (
        times_transposed(preactivation_grad, kernel[1])
        + times_transposed(grad_later, kernel[0])
        + times_transposed(grad_earlier, kernel[2])
    )
    input_grad = (cot_float + activated_output_grad * gelu_slope(inputs)).astype(jnp.bfloat16)
    kernel_grad, offset_grad, mixer_grad, biases_grad = lax.psum(
        (kernel_part, offset_part, mixer_part, biases_part), ("seq", "sub")
    )
    return (layer_output, input_grad, kernel_grad, offset_grad, mixer_grad, biases_grad)


def solution(mesh):
    placed = (P(("seq", "sub"), None), P(), P(), P(), P(), P(("seq", "sub"), None))
    return jax.shard_map(
        local,
        mesh=mesh,
        in_specs=placed,
        out_specs=(P(("seq", "sub"), None), P(("seq", "sub"), None), P(), P(), P(), P()),
        check_vma=False,
    )
```

```python
import math

import jax
import jax.numpy as jnp
from jax import lax
from jax.experimental import pallas as pl
from jax.experimental.pallas import tpu as pltpu
from jax.sharding import PartitionSpec as P

MESH = pl.DeviceIdType.MESH
BF = jnp.bfloat16
F32 = jnp.float32

DILATION_STEP = 8192
C = 768
H = 384
ROWS = 1024
W = 128
NC = H // W
NR = 4
RB = ROWS // NR

NX, NY, NZ = 4, 4, 8

KG1_AT = 0
MG_AT = NC * C
KG02_AT = MG_AT + (H // W) * (C // W) * W
TOTAL = KG02_AT + 2 * NC * C
SEGS = ((0, 4096), (4096, 2048), (6144, 1024), (7168, 2048))
VEC = 16

T_SCALE = 0.3
TAIL = (
    0.11962923731872051,
    0.12075488221323095,
    0.0999078411835699,
    0.12857978094297895,
    -0.05371691656802647,
    0.20638841535029362,
    -0.1572225638776185,
    0.03567924927328374,
)


def gelu_and_slope(v):
    u = jnp.abs(v)
    t = 1.0 / (1.0 + T_SCALE * u)
    poly = TAIL[-1]
    for coef in TAIL[-2::-1]:
        poly = poly * t + coef
    bell = jnp.exp(-0.5 * u * u)
    tail = poly * t * bell
    cdf = jnp.where(v >= 0.0, 1.0 - tail, tail)
    return v * cdf, cdf + v * bell * (1.0 / math.sqrt(2.0 * math.pi))


def nn(a, b):
    return jnp.dot(a, b, preferred_element_type=F32)


def nt(a, b):
    return lax.dot_general(a, b, (((1,), (1,)), ((), ())), preferred_element_type=F32)


def position():
    seq, sub = lax.axis_index("seq"), lax.axis_index("sub")
    z, x = lax.div(seq, 2 * NX), lax.rem(lax.div(seq, 2), NX)
    y = lax.div(sub, 2) * 2 + lax.rem(seq, 2)
    return seq, sub, x, y, z, lax.rem(sub, 2)


def device(x, y, z, core):
    return (z * (2 * NX) + x * 2 + lax.rem(y, 2), lax.div(y, 2) * 2 + core)


def main_kernel(
    f_hbm, k_hbm, off_ref, mix_hbm, bias_ref, cot_hbm,
    lo_hbm, ig_hbm, gg_hbm, vec_ref,
    f_v, cot_v, kw_v, k1_v, mix_v,
    act_v, actt_v, slope_v, pre_v, hg_v,
    t0_v, t2_v, te_v, tl_v, hid_v, hidt_v, pg_v, pg02_v,
    lo_v, ig_v, g_v, sbc, rbc, sby, rby, sbz, rbz, sbx, rbx, gg_v,
    vs, vc, vy, vz, vx,
    f_sem, in_sem, out_sem, halo_send, tap_recv, pg_recv, seg_send, seg_recv, vec_send, vec_recv,
):
    seq, sub, x, y, z, core = position()
    nseq = 2 * NX * NZ
    ahead = (lax.rem(seq + 2, nseq), sub)
    behind = (lax.rem(seq + nseq - 2, nseq), sub)

    def y_peer(d):
        return device(x, lax.rem(y + d, NY), z, core)

    def z_peer(d):
        return device(x, y, lax.rem(z + d, NZ), core)

    def x_peer(d):
        return device(lax.rem(x + d, NX), y, z, core)

    sibling = device(x, y, z, 1 - core)

    barrier = pltpu.get_barrier_semaphore()

    def greet(to):
        pl.semaphore_signal(barrier, inc=1, device_id=to, device_id_type=MESH)

    def greet_loop(n, peer):
        def body(d, carry):
            greet(peer(d))
            return carry

        lax.fori_loop(1, n, body, 0)

    def f_copy(r):
        rows = pl.ds(pl.multiple_of(r * RB, RB), RB)
        return pltpu.make_async_copy(f_hbm.at[rows], f_v.at[rows], f_sem.at[r])

    ins = []
    for c in range(NC):
        lanes = pl.ds(c * W, W)
        ins.append((k_hbm.at[0, :, lanes], kw_v.at[c, :, pl.ds(0, W)]))
        ins.append((k_hbm.at[2, :, lanes], kw_v.at[c, :, pl.ds(W, W)]))
    ins.append((k_hbm.at[1], k1_v))
    ins.append((mix_hbm, mix_v))
    ins.append((cot_hbm, cot_v))
    ins = [pltpu.make_async_copy(s, d, in_sem.at[i]) for i, (s, d) in enumerate(ins)]
    f_copy(0).start()
    ins[0].start()
    ins[1].start()
    for r in range(1, NR):
        f_copy(r).start()
    for copy in ins[2:]:
        copy.start()

    greet(sibling)
    greet(ahead)
    greet(behind)
    greet_loop(NY, y_peer)
    greet_loop(NZ, z_peer)
    greet_loop(NX, x_peer)

    def loop(n, body):
        def step(i, carry):
            body(i)
            return carry

        lax.fori_loop(0, n, step, 0)

    def rows_at(base, i, n):
        return pl.ds(pl.multiple_of(base + i * n, n), n)

    def activate(r):
        def body(i):
            rows = pl.ds(pl.multiple_of(r * RB + i * 16, 16), 16)
            gelu, slope = gelu_and_slope(f_v[rows, :].astype(F32))
            act_v[rows, :] = gelu.astype(BF)
            slope_v[rows, :] = slope

        loop(RB // 16, body)

    def tap_copies(c, r):
        rows = pl.ds(pl.multiple_of(r * RB, RB), RB)
        return (
            pltpu.make_async_remote_copy(
                src_ref=t0_v.at[c, rows], dst_ref=te_v.at[c, rows],
                send_sem=halo_send.at[0], recv_sem=tap_recv.at[0, c, r],
                device_id=ahead, device_id_type=MESH,
            ),
            pltpu.make_async_remote_copy(
                src_ref=t2_v.at[c, rows], dst_ref=tl_v.at[c, rows],
                send_sem=halo_send.at[1], recv_sem=tap_recv.at[1, c, r],
                device_id=behind, device_id_type=MESH,
            ),
        )

    def taps(c, r):
        rows = pl.ds(pl.multiple_of(r * RB, RB), RB)
        both = nn(act_v[rows, :], kw_v[c]).astype(BF)
        t0_v[c, rows, :] = both[:, :W]
        t2_v[c, rows, :] = both[:, W:]

    def send_taps(c, r):
        for copy in tap_copies(c, r):
            copy.start()

    f_copy(0).wait()
    activate(0)
    ins[0].wait()
    ins[1].wait()
    taps(0, 0)
    pl.semaphore_wait(barrier, 1 + 2 + (NY - 1) + (NZ - 1) + (NX - 1))
    send_taps(0, 0)

    def first(i):
        r = i + 1
        f_copy(r).wait()
        activate(r)
        taps(0, r)
        send_taps(0, r)

    loop(NR - 1, first)
    for c in range(1, NC):
        ins[2 * c].wait()
        ins[2 * c + 1].wait()

        def more(r, c=c):
            taps(c, r)
            send_taps(c, r)

        loop(NR, more)

    for copy in ins[2 * NC:]:
        copy.wait()

    def own(r):
        rows = pl.ds(pl.multiple_of(r * RB, RB), RB)
        pre_v[rows, :] = nn(act_v[rows, :], k1_v[...]) + off_ref[...]
        hg_v[rows, :] = nt(cot_v[rows, :], mix_v[...])

    loop(NR, own)

    def pg_copies(c, r):
        rows = pl.ds(pl.multiple_of(r * RB, RB), RB)
        src = pg_v.at[rows, pl.ds(c * W, W)]
        return (
            pltpu.make_async_remote_copy(
                src_ref=src, dst_ref=pg02_v.at[c, rows, pl.ds(0, W)],
                send_sem=halo_send.at[2], recv_sem=pg_recv.at[0, c, r],
                device_id=behind, device_id_type=MESH,
            ),
            pltpu.make_async_remote_copy(
                src_ref=src, dst_ref=pg02_v.at[c, rows, pl.ds(W, W)],
                send_sem=halo_send.at[3], recv_sem=pg_recv.at[1, c, r],
                device_id=ahead, device_id_type=MESH,
            ),
        )

    def hidden(c):
        lanes = slice(c * W, (c + 1) * W)

        def block(r):
            for copy in tap_copies(c, r):
                copy.wait_recv()

            def body(i):
                rows = pl.ds(pl.multiple_of(r * RB + i * 64, 64), 64)
                pre = pre_v[rows, lanes] + te_v[c, rows, :].astype(F32) + tl_v[c, rows, :].astype(F32)
                gelu, slope = gelu_and_slope(pre)
                hid_v[rows, lanes] = gelu.astype(BF)
                pg_v[rows, lanes] = (hg_v[rows, lanes] * slope).astype(BF)

            loop(RB // 64, body)
            for copy in pg_copies(c, r):
                copy.start()

        loop(NR, block)

    CORE, Y, Z, X, GZ, GY, GC = range(7)

    def place(s):
        at, n = SEGS[s]
        half, quarter, part = n // 2, n // 8, n // 64
        own_half = at + core * half
        own_quarter = own_half + y * quarter
        own_part = own_quarter + z * part
        return at, half, quarter, part, own_half, own_quarter, own_part

    def ds(base, n):
        return pl.ds(pl.multiple_of(base, 16), n)

    def send(s, stage, src, dst, to):
        pltpu.make_async_remote_copy(
            src_ref=src, dst_ref=dst, send_sem=seg_send.at[s, stage], recv_sem=seg_recv.at[s, stage],
            device_id=to, device_id_type=MESH,
        ).start()

    def total(s, stage, ref):
        return pltpu.make_async_remote_copy(
            src_ref=ref, dst_ref=ref, send_sem=seg_send.at[s, stage], recv_sem=seg_recv.at[s, stage],
            device_id=sibling, device_id_type=MESH,
        )

    def bulk(s, stage):
        at, half, quarter, part, *_ = place(s)
        if stage in (CORE, GC):
            return rbc.at[pl.ds(at // 2, half)]
        if stage in (Y, GY):
            return rby.at[pl.ds(at // 8 * 3, 3 * quarter)]
        if stage in (Z, GZ):
            return rbz.at[pl.ds(at // 64 * 7, 7 * part)]
        return rbx.at[pl.ds(at // 64 * 4, 3 * part)]

    def core_send(s):
        at, half, *_ = place(s)
        other = at + (1 - core) * half

        def body(i):
            sbc[pl.ds(pl.multiple_of(at // 2 + i * 128, 128), 128), :] = g_v[
                ds(other + i * 128, 128), :
            ].astype(BF)

        loop(half // 128, body)
        rows = pl.ds(at // 2, half)
        send(s, CORE, sbc.at[rows], rbc.at[rows], sibling)

    def y_send(s):
        at, half, quarter, part, own_half, own_quarter, own_part = place(s)
        total(s, CORE, bulk(s, CORE)).wait_recv()

        def body(i):
            rows = ds(own_half + i * 128, 128)
            got = pl.ds(pl.multiple_of(at // 2 + i * 128, 128), 128)
            summed = g_v[rows, :] + rbc[got, :].astype(F32)
            g_v[rows, :] = summed
            sby[got, :] = summed.astype(BF)

        loop(half // 128, body)

        def to(d, carry):
            ty = lax.rem(y + d, NY)
            send(
                s, Y, sby.at[ds(at // 2 + ty * quarter, quarter)],
                rby.at[ds(at // 8 * 3 + (d - 1) * quarter, quarter)], y_peer(d),
            )
            return carry

        lax.fori_loop(1, NY, to, 0)

    def z_send(s):
        at, half, quarter, part, own_half, own_quarter, own_part = place(s)
        total(s, Y, bulk(s, Y)).wait_recv()

        def body(i):
            rows = ds(own_quarter + i * 64, 64)
            summed = g_v[rows, :]
            for d in range(NY - 1):
                summed = summed + rby[ds(at // 8 * 3 + d * quarter + i * 64, 64), :].astype(F32)
            g_v[rows, :] = summed
            sbz[ds(at // 8 + i * 64, 64), :] = summed.astype(BF)

        loop(quarter // 64, body)

        def to(d, carry):
            tz = lax.rem(z + d, NZ)
            send(
                s, Z, sbz.at[ds(at // 8 + tz * part, part)],
                rbz.at[ds(at // 64 * 7 + (d - 1) * part, part)], z_peer(d),
            )
            return carry

        lax.fori_loop(1, NZ, to, 0)

    def x_send(s):
        at, half, quarter, part, own_half, own_quarter, own_part = place(s)
        total(s, Z, bulk(s, Z)).wait_recv()
        summed = g_v[ds(own_part, part), :]
        for d in range(NZ - 1):
            summed = summed + rbz[ds(at // 64 * 7 + d * part, part), :].astype(F32)
        mine = rbx.at[ds(at // 64 * 4 + x * part, part)]
        sbx[pl.ds(at // 64, part), :] = summed.astype(BF)
        rbx[ds(at // 64 * 4 + x * part, part), :] = summed.astype(BF)

        def to(d, carry):
            send(s, X, sbx.at[pl.ds(at // 64, part)], mine, x_peer(d))
            return carry

        lax.fori_loop(1, NX, to, 0)

    def z_gather(s):
        at, half, quarter, part, own_half, own_quarter, own_part = place(s)
        total(s, X, bulk(s, X)).wait_recv()
        summed = rbx[pl.ds(at // 64 * 4, part), :].astype(F32)
        for k in range(1, NX):
            summed = summed + rbx[pl.ds(at // 64 * 4 + k * part, part), :].astype(F32)
        gg_v[ds(own_part, part), :] = summed.astype(BF)
        ref = gg_v.at[ds(own_part, part)]

        def to(d, carry):
            send(s, GZ, ref, ref, z_peer(d))
            return carry

        lax.fori_loop(1, NZ, to, 0)

    def y_gather(s):
        at, half, quarter, part, own_half, own_quarter, own_part = place(s)
        total(s, GZ, bulk(s, GZ)).wait_recv()
        ref = gg_v.at[ds(own_quarter, quarter)]

        def to(d, carry):
            send(s, GY, ref, ref, y_peer(d))
            return carry

        lax.fori_loop(1, NY, to, 0)

    def core_gather(s):
        at, half, quarter, part, own_half, own_quarter, own_part = place(s)
        total(s, GY, bulk(s, GY)).wait_recv()
        ref = gg_v.at[ds(own_half, half)]
        send(s, GC, ref, ref, sibling)

    def out_copy(s):
        at, n = SEGS[s]
        rows = pl.ds(at, n)
        return pltpu.make_async_copy(gg_v.at[rows], gg_hbm.at[rows], out_sem.at[2 + s])

    def finish(s):
        total(s, GC, bulk(s, GC)).wait_recv()
        out_copy(s).start()

    vec_stages = ((vc, 2, core, lambda d: sibling), (vy, NY, y, y_peer), (vz, NZ, z, z_peer), (vx, NX, x, x_peer))

    def vec_all(stage):
        ref, n, _, _ = vec_stages[stage]
        whole = ref.at[pl.ds(0, n - 1)]
        return pltpu.make_async_remote_copy(
            src_ref=whole, dst_ref=whole, send_sem=vec_send.at[stage], recv_sem=vec_recv.at[stage],
            device_id=sibling, device_id_type=MESH,
        )

    def vec_step(stage):
        if stage == 0:
            value = vs[0]
        else:
            vec_all(stage - 1).wait_recv()
            before, n, _, _ = vec_stages[stage - 1]
            value = before[0]
            for k in range(1, n):
                value = value + before[k]
        if stage == len(vec_stages):
            vec_ref[...] = value
            return
        ref, n, me, peer = vec_stages[stage]
        vs[stage] = value
        ref[me] = value

        def to(d, carry):
            pltpu.make_async_remote_copy(
                src_ref=vs.at[stage], dst_ref=ref.at[me],
                send_sem=vec_send.at[stage], recv_sem=vec_recv.at[stage],
                device_id=peer(d), device_id_type=MESH,
            ).start()
            return carry

        lax.fori_loop(1, n, to, 0)

    def transpose(r):
        for r in range(NR):
            rows = pl.ds(r * RB, RB)
            actt_v[:, rows] = act_v[rows, :].T

    hidden(0)
    transpose(0)
    hidden(1)
    hidden(2)

    for r in range(NR):
        rows = pl.ds(r * RB, RB)
        hidt_v[:, rows] = hid_v[rows, :].T

    def kg1(m):
        part = nn(actt_v[pl.ds(pl.multiple_of(m * 256, 256), 256), :], pg_v[...])
        for c in range(NC):
            g_v[pl.ds(pl.multiple_of(KG1_AT + c * C + m * 256, 256), 256), :] = part[:, c * W:(c + 1) * W]

    loop(C // 256, kg1)
    for j in range(C // 256):
        part = nn(hidt_v[...], cot_v[:, j * 256:(j + 1) * 256])
        for c in range(H // W):
            for k in range(2):
                at = MG_AT + (c * (C // W) + j * 2 + k) * W
                g_v[pl.ds(at, W), :] = part[c * W:(c + 1) * W, k * W:(k + 1) * W]

    core_send(0)
    ones = jnp.ones((8, ROWS), BF)
    cot_sum = nn(ones, cot_v[...])
    pg_sum = nn(ones, pg_v[...])
    for j in range(C // W):
        vs[0, j:j + 1, :] = cot_sum[:1, j * W:(j + 1) * W]
    for j in range(H // W):
        vs[0, C // W + j:C // W + j + 1, :] = pg_sum[:1, j * W:(j + 1) * W]
    done = C // W + H // W
    vs[0, done:, :] = jnp.zeros((VEC - done, W), F32)
    vec_step(0)

    def kg02(c):
        def wait(r):
            for copy in pg_copies(c, r):
                copy.wait_recv()

        loop(NR, wait)

        def block(m):
            part = nn(actt_v[pl.ds(pl.multiple_of(m * 256, 256), 256), :], pg02_v[c])
            at = KG02_AT + c * 2 * C + m * 256
            g_v[pl.ds(pl.multiple_of(at, 256), 256), :] = part[:, :W]
            g_v[pl.ds(pl.multiple_of(at + C, 256), 256), :] = part[:, W:]

        loop(C // 256, block)

    def leave(r):
        rows = pl.ds(pl.multiple_of(r * RB, RB), RB)
        lo_v[rows, :] = (f_v[rows, :].astype(F32) + nn(hid_v[rows, :], mix_v[...]) + bias_ref[...]).astype(BF)

    y_send(0)
    vec_step(1)
    loop(NR, leave)
    lo_copy = pltpu.make_async_copy(lo_v, lo_hbm, out_sem.at[0])
    lo_copy.start()
    kg02(0)
    core_send(1)
    z_send(0)
    vec_step(2)
    y_send(1)
    x_send(0)
    vec_step(3)
    kg02(1)
    core_send(2)
    z_gather(0)
    vec_step(4)
    z_send(1)
    y_send(2)
    kg02(2)
    core_send(3)
    y_gather(0)
    x_send(1)
    z_send(2)
    y_send(3)

    def grad_in(r):
        rows = pl.ds(pl.multiple_of(r * RB, RB), RB)
        grad = nt(pg_v[rows, :], k1_v[...])
        for c in range(NC):
            grad = grad + nt(pg02_v[c, rows, :], kw_v[c])
        ig_v[rows, :] = (cot_v[rows, :].astype(F32) + grad * slope_v[rows, :]).astype(BF)

    loop(2, grad_in)
    core_gather(0)
    z_gather(1)
    x_send(2)
    z_send(3)
    loop(2, lambda i: grad_in(i + 2))
    ig_copy = pltpu.make_async_copy(ig_v, ig_hbm, out_sem.at[1])
    ig_copy.start()
    y_gather(1)
    z_gather(2)
    x_send(3)
    finish(0)
    core_gather(1)
    y_gather(2)
    z_gather(3)
    finish(1)
    core_gather(2)
    y_gather(3)
    finish(2)
    core_gather(3)
    finish(3)

    for d, ref in ((0, t0_v), (1, t2_v), (2, t0_v), (3, t2_v)):
        pltpu.make_async_remote_copy(
            src_ref=ref, dst_ref=ref, send_sem=halo_send.at[d], recv_sem=tap_recv.at[0, 0, 0],
            device_id=sibling, device_id_type=MESH,
        ).wait_send()
    for stage in range(len(vec_stages)):
        vec_all(stage).wait_send()
    for s in range(len(SEGS)):
        for stage in range(7):
            total(s, stage, bulk(s, stage)).wait_send()
    lo_copy.wait()
    ig_copy.wait()
    for s in range(len(SEGS)):
        out_copy(s).wait()


def finish_kernel(factor, lo_in, ig_in, gg_in, lo_out, ig_out, kg_out, mg_out, gg_v, kg_v, mg_v, sem):
    copies = [
        pltpu.make_async_copy(lo_in, lo_out, sem.at[0]),
        pltpu.make_async_copy(ig_in, ig_out, sem.at[1]),
    ]
    load = [
        pltpu.make_async_copy(
            gg_in.at[pl.ds(at, n)], gg_v.at[pl.ds(at, n)], sem.at[2 + i]
        )
        for i, (at, n) in enumerate(((KG1_AT, NC * C), (MG_AT, NC * C), (KG02_AT, 2 * NC * C)))
    ]
    for copy in load + copies:
        copy.start()
    stores = [pltpu.make_async_copy(kg_v.at[k], kg_out.at[k], sem.at[5 + k]) for k in range(3)]
    stores.append(pltpu.make_async_copy(mg_v, mg_out, sem.at[8]))

    def spread(k, starts):
        for c in range(NC):
            def body(i, carry, c=c):
                rows = pl.ds(pl.multiple_of(i * 128, 128), 128)
                source = pl.ds(pl.multiple_of(starts[c] + i * 128, 128), 128)
                kg_v[k, rows, c * W:(c + 1) * W] = gg_v[source, :].astype(F32) * factor
                return carry

            lax.fori_loop(0, C // 128, body, 0)
        stores[k].start()

    load[0].wait()
    spread(1, [KG1_AT + c * C for c in range(NC)])
    load[1].wait()
    for c in range(H // W):
        for j in range(C // W):
            at = MG_AT + (c * (C // W) + j) * W
            mg_v[c * W:(c + 1) * W, j * W:(j + 1) * W] = gg_v[at:at + W, :].astype(F32) * factor
    stores[3].start()
    load[2].wait()
    spread(0, [KG02_AT + c * 2 * C for c in range(NC)])
    spread(2, [KG02_AT + c * 2 * C + C for c in range(NC)])
    for copy in copies + stores:
        copy.wait()


def local(features, kernel, offsets, mixer, biases, cotangent):
    length = features.shape[0] * lax.axis_size("seq") * lax.axis_size("sub")
    factor = 1.0 / math.sqrt(length)
    any_spec = pl.BlockSpec(memory_space=pl.ANY)
    vmem_spec = pl.BlockSpec(memory_space=pltpu.VMEM)
    n = len(SEGS)
    vm = pltpu.VMEM
    dma = pltpu.SemaphoreType.DMA
    lo, ig, gg, vec = pl.pallas_call(
        main_kernel,
        out_shape=(
            jax.ShapeDtypeStruct((ROWS, C), BF),
            jax.ShapeDtypeStruct((ROWS, C), BF),
            jax.ShapeDtypeStruct((TOTAL, W), BF),
            jax.ShapeDtypeStruct((VEC, W), F32),
        ),
        in_specs=[any_spec, any_spec, vmem_spec, any_spec, vmem_spec, any_spec],
        out_specs=(any_spec, any_spec, any_spec, vmem_spec),
        scratch_shapes=[
            vm((ROWS, C), BF), vm((ROWS, C), BF), vm((NC, C, 2 * W), BF), vm((C, H), BF), vm((H, C), BF),
            vm((ROWS, C), BF), vm((C, ROWS), BF), vm((ROWS, C), F32), vm((ROWS, H), F32), vm((ROWS, H), F32),
            vm((NC, ROWS, W), BF), vm((NC, ROWS, W), BF), vm((NC, ROWS, W), BF), vm((NC, ROWS, W), BF),
            vm((ROWS, H), BF), vm((H, ROWS), BF), vm((ROWS, H), BF), vm((NC, ROWS, 2 * W), BF),
            vm((ROWS, C), BF), vm((ROWS, C), BF), vm((TOTAL, W), F32),
            vm((TOTAL // 2, W), BF), vm((TOTAL // 2, W), BF), vm((TOTAL // 2, W), BF), vm((TOTAL // 8 * 3, W), BF),
            vm((TOTAL // 8, W), BF), vm((TOTAL // 64 * 7, W), BF), vm((TOTAL // 64, W), BF),
            vm((TOTAL // 64 * 4, W), BF), vm((TOTAL, W), BF),
            vm((4, VEC, W), F32), vm((2, VEC, W), F32), vm((NY, VEC, W), F32), vm((NZ, VEC, W), F32),
            vm((NX, VEC, W), F32),
            dma((NR,)), dma((2 * NC + 3,)), dma((2 + n,)), dma((4,)), dma((2, NC, NR)), dma((2, NC, NR)),
            dma((n, 7)), dma((n, 7)), dma((4,)), dma((4,)),
        ],
        compiler_params=pltpu.CompilerParams(
            collective_id=0, has_side_effects=True, vmem_limit_bytes=60 * 2**20
        ),
        cost_estimate=pl.CostEstimate(flops=8_000_000_000, bytes_accessed=16_000_000, transcendentals=1_200_000),
        name="block",
    )(features, kernel, offsets.reshape(1, H), mixer, biases.reshape(1, C), cotangent)
    layer_output, input_grad, kernel_grad, mixer_grad = pl.pallas_call(
        lambda *refs: finish_kernel(factor, *refs),
        out_shape=(
            jax.ShapeDtypeStruct((ROWS, C), BF),
            jax.ShapeDtypeStruct((ROWS, C), BF),
            jax.ShapeDtypeStruct((3, C, H), F32),
            jax.ShapeDtypeStruct((H, C), F32),
        ),
        in_specs=[any_spec] * 3,
        out_specs=(any_spec,) * 4,
        scratch_shapes=[vm((TOTAL, W), BF), vm((3, C, H), F32), vm((H, C), F32), dma((9,))],
        compiler_params=pltpu.CompilerParams(vmem_limit_bytes=24 * 2**20),
        name="finish",
    )(lo, ig, gg)
    sums = vec.reshape(VEC * W) * factor
    return (layer_output, input_grad, kernel_grad, sums[C:C + H], mixer_grad, sums[:C])


def solution(mesh):
    placed = (P(("seq", "sub"), None), P(), P(), P(), P(), P(("seq", "sub"), None))
    return jax.shard_map(
        local,
        mesh=mesh,
        in_specs=placed,
        out_specs=(P(("seq", "sub"), None), P(("seq", "sub"), None), P(), P(), P(), P()),
        check_vma=False,
    )
```

```python
import math

import jax
import jax.numpy as jnp
from jax import lax
from jax.experimental import pallas as pl
from jax.experimental.pallas import tpu as pltpu
from jax.sharding import PartitionSpec as P

MESH = pl.DeviceIdType.MESH
BF = jnp.bfloat16
F32 = jnp.float32

DILATION_STEP = 8192
C = 768
H = 384
ROWS = 1024
W = 128
NC = H // W
NR = 4
RB = ROWS // NR

NX, NY, NZ = 4, 4, 8

PAIR = 2 * C
KG1_AT, MG_AT, KG02_AT = 0, C, NC * PAIR
TOTAL = 2 * NC * PAIR
SEGS = ((0, 3072), (3072, 3072), (6144, 1024), (7168, 2048))
LAST = len(SEGS) - 1
NP = NX * NY
SHARE = SEGS[LAST][1] // (2 * NP)
SLICE = SHARE // NZ
VEC = 16

T_SCALE = 0.3
TAIL = (
    0.11962923731872051,
    0.12075488221323095,
    0.0999078411835699,
    0.12857978094297895,
    -0.05371691656802647,
    0.20638841535029362,
    -0.1572225638776185,
    0.03567924927328374,
)


def gelu_and_slope(v):
    u = jnp.abs(v)
    t = 1.0 / (1.0 + T_SCALE * u)
    poly = TAIL[-1]
    for coef in TAIL[-2::-1]:
        poly = poly * t + coef
    bell = jnp.exp(-0.5 * u * u)
    tail = poly * t * bell
    cdf = jnp.where(v >= 0.0, 1.0 - tail, tail)
    return v * cdf, cdf + v * bell * (1.0 / math.sqrt(2.0 * math.pi))


def nn(a, b):
    return jnp.dot(a, b, preferred_element_type=F32)


def nt(a, b):
    return lax.dot_general(a, b, (((1,), (1,)), ((), ())), preferred_element_type=F32)


def position():
    seq, sub = lax.axis_index("seq"), lax.axis_index("sub")
    z, x = lax.div(seq, 2 * NX), lax.rem(lax.div(seq, 2), NX)
    y = lax.div(sub, 2) * 2 + lax.rem(seq, 2)
    return seq, sub, x, y, z, lax.rem(sub, 2)


def device(x, y, z, core):
    return (z * (2 * NX) + x * 2 + lax.rem(y, 2), lax.div(y, 2) * 2 + core)


def main_kernel(
    f_hbm, k_hbm, off_hbm, mix_hbm, bias_hbm, cot_hbm,
    lo_v, ig_v, gg_v, vec_ref,
    f_v, cot_v, kw_v, k1_v, mix_v, off_v, bias_v,
    act_v, actt_v, slope_v, pre_v, hg_v,
    t0_v, t2_v, te_v, tl_v, hid_v, hidt_v, pg_v, pg02_v,
    g_v, sbc, rbc, sby, rby, sbz, rbz, sbx, rbx,
    last_s, last_r, last_own, last_zs, last_zr, last_g,
    vs, vc, vy, vz, vx,
    f_sem, in_sem, halo_send, tap_recv, pg_recv, seg_send, seg_recv, vec_send, vec_recv,
):
    seq, sub, x, y, z, core = position()
    nseq = 2 * NX * NZ
    ahead = (lax.rem(seq + 2, nseq), sub)
    behind = (lax.rem(seq + nseq - 2, nseq), sub)

    def y_peer(d):
        return device(x, lax.rem(y + d, NY), z, core)

    def z_peer(d):
        return device(x, y, lax.rem(z + d, NZ), core)

    def x_peer(d):
        return device(lax.rem(x + d, NX), y, z, core)

    def xy_at(d):
        return lax.rem(x * NY + y + d, NP)

    def xy_peer(d):
        return device(lax.div(xy_at(d), NY), lax.rem(xy_at(d), NY), z, core)

    sibling = device(x, y, z, 1 - core)

    barrier = pltpu.get_barrier_semaphore()

    def greet(to):
        pl.semaphore_signal(barrier, inc=1, device_id=to, device_id_type=MESH)

    def greet_loop(n, peer):
        def body(d, carry):
            greet(peer(d))
            return carry

        lax.fori_loop(1, n, body, 0)

    def f_copy(r):
        rows = pl.ds(pl.multiple_of(r * RB, RB), RB)
        return pltpu.make_async_copy(f_hbm.at[rows], f_v.at[rows], f_sem.at[r])

    ins = []
    for c in range(NC):
        lanes = pl.ds(c * W, W)
        ins.append((k_hbm.at[0, :, lanes], kw_v.at[c, :, pl.ds(0, W)]))
        ins.append((k_hbm.at[2, :, lanes], kw_v.at[c, :, pl.ds(W, W)]))
    ins.append((k_hbm.at[1], k1_v))
    ins.append((mix_hbm, mix_v))
    ins.append((cot_hbm, cot_v))
    ins.append((off_hbm, off_v))
    ins.append((bias_hbm, bias_v))
    ins = [pltpu.make_async_copy(s, d, in_sem.at[i]) for i, (s, d) in enumerate(ins)]
    f_copy(0).start()
    ins[0].start()
    ins[1].start()
    for r in range(1, NR):
        f_copy(r).start()
    for copy in ins[2:]:
        copy.start()

    greet(sibling)
    greet(ahead)
    greet(behind)
    greet_loop(NP, xy_peer)
    greet_loop(NZ, z_peer)

    def loop(n, body):
        def step(i, carry):
            body(i)
            return carry

        lax.fori_loop(0, n, step, 0)

    def rows_at(base, i, n):
        return pl.ds(pl.multiple_of(base + i * n, n), n)

    def activate(r):
        def body(i):
            rows = pl.ds(pl.multiple_of(r * RB + i * 16, 16), 16)
            gelu, slope = gelu_and_slope(f_v[rows, :].astype(F32))
            act_v[rows, :] = gelu.astype(BF)
            slope_v[rows, :] = slope

        loop(RB // 16, body)

    def tap_copies(c, r):
        rows = pl.ds(pl.multiple_of(r * RB, RB), RB)
        return (
            pltpu.make_async_remote_copy(
                src_ref=t0_v.at[c, rows], dst_ref=te_v.at[c, rows],
                send_sem=halo_send.at[0], recv_sem=tap_recv.at[0, c, r],
                device_id=ahead, device_id_type=MESH,
            ),
            pltpu.make_async_remote_copy(
                src_ref=t2_v.at[c, rows], dst_ref=tl_v.at[c, rows],
                send_sem=halo_send.at[1], recv_sem=tap_recv.at[1, c, r],
                device_id=behind, device_id_type=MESH,
            ),
        )

    def taps(c, r):
        rows = pl.ds(pl.multiple_of(r * RB, RB), RB)
        both = nn(act_v[rows, :], kw_v[c]).astype(BF)
        t0_v[c, rows, :] = both[:, :W]
        t2_v[c, rows, :] = both[:, W:]

    def send_taps(c, r):
        for copy in tap_copies(c, r):
            copy.start()

    with jax.named_scope("start"):
        f_copy(0).wait()
        activate(0)
        ins[0].wait()
        ins[1].wait()
        taps(0, 0)
    with jax.named_scope("greeted"):
        pl.semaphore_wait(barrier, 1 + 2 + (NP - 1) + (NZ - 1))
    send_taps(0, 0)

    def first(i):
        r = i + 1
        f_copy(r).wait()
        activate(r)
        taps(0, r)
        send_taps(0, r)

    with jax.named_scope("first"):
        loop(NR - 1, first)
    for c in range(1, NC):
        ins[2 * c].wait()
        ins[2 * c + 1].wait()

        def more(r, c=c):
            taps(c, r)
            send_taps(c, r)

        with jax.named_scope("more_taps"):
            loop(NR, more)

    for copy in ins[2 * NC:]:
        copy.wait()

    def own(r):
        rows = pl.ds(pl.multiple_of(r * RB, RB), RB)
        pre_v[rows, :] = nn(act_v[rows, :], k1_v[...]) + off_v[...].reshape(1, H)
        hg_v[rows, :] = nt(cot_v[rows, :], mix_v[...])

    with jax.named_scope("own"):
        loop(NR, own)

    def pg_copies(c, r):
        rows = pl.ds(pl.multiple_of(r * RB, RB), RB)
        src = pg_v.at[rows, pl.ds(c * W, W)]
        return (
            pltpu.make_async_remote_copy(
                src_ref=src, dst_ref=pg02_v.at[c, rows, pl.ds(0, W)],
                send_sem=halo_send.at[2], recv_sem=pg_recv.at[0, c, r],
                device_id=behind, device_id_type=MESH,
            ),
            pltpu.make_async_remote_copy(
                src_ref=src, dst_ref=pg02_v.at[c, rows, pl.ds(W, W)],
                send_sem=halo_send.at[3], recv_sem=pg_recv.at[1, c, r],
                device_id=ahead, device_id_type=MESH,
            ),
        )

    def hidden(c, first=0, last=NR):
        lanes = slice(c * W, (c + 1) * W)

        def block(r):
            for copy in tap_copies(c, r):
                copy.wait_recv()

            def body(i):
                rows = pl.ds(pl.multiple_of(r * RB + i * 64, 64), 64)
                pre = pre_v[rows, lanes] + te_v[c, rows, :].astype(F32) + tl_v[c, rows, :].astype(F32)
                gelu, slope = gelu_and_slope(pre)
                hid_v[rows, lanes] = gelu.astype(BF)
                pg_v[rows, lanes] = (hg_v[rows, lanes] * slope).astype(BF)

            loop(RB // 64, body)
            for copy in pg_copies(c, r):
                copy.start()

        loop(last - first, lambda i: block(first + i))

    CORE, Y, Z, X, GZ, GY, GC = range(7)

    def place(s):
        at, n = SEGS[s]
        half, quarter, part = n // 2, n // 8, n // 64
        own_half = at + core * half
        own_quarter = own_half + y * quarter
        own_part = own_quarter + z * part
        return at, half, quarter, part, own_half, own_quarter, own_part

    def ds(base, n):
        return pl.ds(pl.multiple_of(base, 16), n)

    def send(s, stage, src, dst, to):
        pltpu.make_async_remote_copy(
            src_ref=src, dst_ref=dst, send_sem=seg_send.at[s, stage], recv_sem=seg_recv.at[s, stage],
            device_id=to, device_id_type=MESH,
        ).start()

    def total(s, stage, ref):
        return pltpu.make_async_remote_copy(
            src_ref=ref, dst_ref=ref, send_sem=seg_send.at[s, stage], recv_sem=seg_recv.at[s, stage],
            device_id=sibling, device_id_type=MESH,
        )

    def bulk(s, stage):
        at, half, quarter, part, *_ = place(s)
        if s == LAST and stage in (Y, GY):
            return last_r
        if s == LAST and stage in (Z, GZ):
            return last_zr
        if stage in (CORE, GC):
            return rbc.at[pl.ds(at // 2, half)]
        if stage in (Y, GY):
            return rby.at[pl.ds(at // 8 * 3, 3 * quarter)]
        if stage in (Z, GZ):
            return rbz.at[pl.ds(at // 64 * 7, 7 * part)]
        return rbx.at[pl.ds(at // 64 * 4, 3 * part)]

    def core_send(s):
        at, half, *_ = place(s)
        other = at + (1 - core) * half

        def body(i):
            sbc[pl.ds(pl.multiple_of(at // 2 + i * 128, 128), 128), :] = g_v[
                ds(other + i * 128, 128), :
            ].astype(BF)

        loop(half // 128, body)
        rows = pl.ds(at // 2, half)
        send(s, CORE, sbc.at[rows], rbc.at[rows], sibling)

    def y_send(s):
        at, half, quarter, part, own_half, own_quarter, own_part = place(s)
        total(s, CORE, bulk(s, CORE)).wait_recv()

        def body(i):
            rows = ds(own_half + i * 128, 128)
            got = pl.ds(pl.multiple_of(at // 2 + i * 128, 128), 128)
            summed = g_v[rows, :] + rbc[got, :].astype(F32)
            g_v[rows, :] = summed
            sby[got, :] = summed.astype(BF)

        loop(half // 128, body)

        def to(d, carry):
            ty = lax.rem(y + d, NY)
            send(
                s, Y, sby.at[ds(at // 2 + ty * quarter, quarter)],
                rby.at[ds(at // 8 * 3 + (d - 1) * quarter, quarter)], y_peer(d),
            )
            return carry

        lax.fori_loop(1, NY, to, 0)

    def z_send(s):
        at, half, quarter, part, own_half, own_quarter, own_part = place(s)
        total(s, Y, bulk(s, Y)).wait_recv()

        def body(i):
            rows = ds(own_quarter + i * 64, 64)
            summed = g_v[rows, :]
            for d in range(NY - 1):
                summed = summed + rby[ds(at // 8 * 3 + d * quarter + i * 64, 64), :].astype(F32)
            g_v[rows, :] = summed
            sbz[ds(at // 8 + i * 64, 64), :] = summed.astype(BF)

        loop(quarter // 64, body)

        def to(d, carry):
            tz = lax.rem(z + d, NZ)
            send(
                s, Z, sbz.at[ds(at // 8 + tz * part, part)],
                rbz.at[ds(at // 64 * 7 + (d - 1) * part, part)], z_peer(d),
            )
            return carry

        lax.fori_loop(1, NZ, to, 0)

    def x_send(s):
        at, half, quarter, part, own_half, own_quarter, own_part = place(s)
        total(s, Z, bulk(s, Z)).wait_recv()
        summed = g_v[ds(own_part, part), :]
        for d in range(NZ - 1):
            summed = summed + rbz[ds(at // 64 * 7 + d * part, part), :].astype(F32)
        mine = rbx.at[ds(at // 64 * 4 + x * part, part)]
        sbx[pl.ds(at // 64, part), :] = summed.astype(BF)
        rbx[ds(at // 64 * 4 + x * part, part), :] = summed.astype(BF)

        def to(d, carry):
            send(s, X, sbx.at[pl.ds(at // 64, part)], mine, x_peer(d))
            return carry

        lax.fori_loop(1, NX, to, 0)

    def z_gather(s):
        at, half, quarter, part, own_half, own_quarter, own_part = place(s)
        total(s, X, bulk(s, X)).wait_recv()
        summed = rbx[pl.ds(at // 64 * 4, part), :].astype(F32)
        for k in range(1, NX):
            summed = summed + rbx[pl.ds(at // 64 * 4 + k * part, part), :].astype(F32)
        gg_v[ds(own_part, part), :] = summed.astype(BF)
        ref = gg_v.at[ds(own_part, part)]

        def to(d, carry):
            send(s, GZ, ref, ref, z_peer(d))
            return carry

        lax.fori_loop(1, NZ, to, 0)

    def y_gather(s):
        at, half, quarter, part, own_half, own_quarter, own_part = place(s)
        total(s, GZ, bulk(s, GZ)).wait_recv()
        ref = gg_v.at[ds(own_quarter, quarter)]

        def to(d, carry):
            send(s, GY, ref, ref, y_peer(d))
            return carry

        lax.fori_loop(1, NY, to, 0)

    def core_gather(s):
        at, half, quarter, part, own_half, own_quarter, own_part = place(s)
        total(s, GY, bulk(s, GY)).wait_recv()
        ref = gg_v.at[ds(own_half, half)]
        send(s, GC, ref, ref, sibling)

    last_half = SEGS[LAST][0] + core * (SEGS[LAST][1] // 2)

    def last_xy():
        at, half, *_ = place(LAST)
        total(LAST, CORE, bulk(LAST, CORE)).wait_recv()

        def body(i):
            rows = ds(last_half + i * SHARE, SHARE)
            got = pl.ds(pl.multiple_of(at // 2 + i * SHARE, SHARE), SHARE)
            summed = g_v[rows, :] + rbc[got, :].astype(F32)
            g_v[rows, :] = summed
            last_s[i] = summed.astype(BF)

        loop(NP, body)

        def to(d, carry):
            send(LAST, Y, last_s.at[xy_at(d)], last_r.at[d - 1], xy_peer(d))
            return carry

        lax.fori_loop(1, NP, to, 0)

    def last_z():
        total(LAST, Y, last_r).wait_recv()
        summed = g_v[ds(last_half + xy_at(0) * SHARE, SHARE), :]
        for d in range(NP - 1):
            summed = summed + last_r[d].astype(F32)
        summed = summed.reshape(NZ, SLICE, W)
        last_own[...] = summed
        last_zs[...] = summed.astype(BF)

        def to(d, carry):
            send(LAST, Z, last_zs.at[lax.rem(z + d, NZ)], last_zr.at[d - 1], z_peer(d))
            return carry

        lax.fori_loop(1, NZ, to, 0)

    def last_z_gather():
        total(LAST, Z, last_zr).wait_recv()
        summed = last_own[z]
        for d in range(NZ - 1):
            summed = summed + last_zr[d].astype(F32)
        last_g[z] = summed.astype(BF)
        ref = last_g.at[z]

        def to(d, carry):
            send(LAST, GZ, ref, ref, z_peer(d))
            return carry

        lax.fori_loop(1, NZ, to, 0)

    def last_xy_gather():
        total(LAST, GZ, last_zr).wait_recv()
        rows = ds(last_half + xy_at(0) * SHARE, SHARE)
        gg_v[rows, :] = last_g[...].astype(F32).reshape(SHARE, W).astype(BF)
        ref = gg_v.at[rows]

        def to(d, carry):
            send(LAST, GY, ref, ref, xy_peer(d))
            return carry

        lax.fori_loop(1, NP, to, 0)

    def finish(s):
        total(s, GC, bulk(s, GC)).wait_recv()

    vec_stages = ((vc, 2, core, lambda d: sibling), (vy, NY, y, y_peer), (vz, NZ, z, z_peer), (vx, NX, x, x_peer))

    def vec_all(stage):
        ref, n, _, _ = vec_stages[stage]
        whole = ref.at[pl.ds(0, n - 1)]
        return pltpu.make_async_remote_copy(
            src_ref=whole, dst_ref=whole, send_sem=vec_send.at[stage], recv_sem=vec_recv.at[stage],
            device_id=sibling, device_id_type=MESH,
        )

    def vec_step(stage):
        if stage == 0:
            value = vs[0]
        else:
            vec_all(stage - 1).wait_recv()
            before, n, _, _ = vec_stages[stage - 1]
            value = before[0]
            for k in range(1, n):
                value = value + before[k]
        if stage == len(vec_stages):
            vec_ref[...] = value
            return
        ref, n, me, peer = vec_stages[stage]
        vs[stage] = value
        ref[me] = value

        def to(d, carry):
            pltpu.make_async_remote_copy(
                src_ref=vs.at[stage], dst_ref=ref.at[me],
                send_sem=vec_send.at[stage], recv_sem=vec_recv.at[stage],
                device_id=peer(d), device_id_type=MESH,
            ).start()
            return carry

        lax.fori_loop(1, n, to, 0)

    def transpose(r):
        for r in range(NR):
            rows = pl.ds(r * RB, RB)
            actt_v[:, rows] = act_v[rows, :].T

    def kg1_and_mixer(c, n):
        lanes = slice(c * W, (c + n) * W)
        for r in range(NR):
            rows = pl.ds(r * RB, RB)
            hidt_v[lanes, rows] = hid_v[rows, lanes].T

        def kg1(m):
            part = nn(actt_v[pl.ds(pl.multiple_of(m * 256, 256), 256), :], pg_v[:, lanes])
            for k in range(n):
                at = KG1_AT + (c + k) * PAIR + m * 256
                g_v[pl.ds(pl.multiple_of(at, 256), 256), :] = part[:, k * W:(k + 1) * W]

        loop(C // 256, kg1)
        for j in range(C // 256):
            part = nn(hidt_v[lanes, :], cot_v[:, j * 256:(j + 1) * 256])
            for i in range(n):
                for k in range(2):
                    at = MG_AT + (c + i) * PAIR + (j * 2 + k) * W
                    g_v[pl.ds(at, W), :] = part[i * W:(i + 1) * W, k * W:(k + 1) * W]

    def vectors():
        ones = jnp.ones((8, ROWS), BF)
        cot_sum = nn(ones, cot_v[...])
        pg_sum = nn(ones, pg_v[...])
        for j in range(C // W):
            vs[0, j:j + 1, :] = cot_sum[:1, j * W:(j + 1) * W]
        for j in range(H // W):
            vs[0, C // W + j:C // W + j + 1, :] = pg_sum[:1, j * W:(j + 1) * W]
        done = C // W + H // W
        vs[0, done:, :] = jnp.zeros((VEC - done, W), F32)

    def kg02(c):
        def wait(r):
            for copy in pg_copies(c, r):
                copy.wait_recv()

        loop(NR, wait)

        def block(m):
            part = nn(actt_v[pl.ds(pl.multiple_of(m * 256, 256), 256), :], pg02_v[c])
            at = KG02_AT + c * PAIR + m * 256
            g_v[pl.ds(pl.multiple_of(at, 256), 256), :] = part[:, :W]
            g_v[pl.ds(pl.multiple_of(at + C, 256), 256), :] = part[:, W:]

        loop(C // 256, block)

    def leave(r):
        rows = pl.ds(pl.multiple_of(r * RB, RB), RB)
        lo_v[rows, :] = (f_v[rows, :].astype(F32) + nn(hid_v[rows, :], mix_v[...]) + bias_v[...].reshape(1, C)).astype(BF)

    def grad_in(r):
        rows = pl.ds(pl.multiple_of(r * RB, RB), RB)
        grad = nt(pg_v[rows, :], k1_v[...])
        for c in range(NC):
            grad = grad + nt(pg02_v[c, rows, :], kw_v[c])
        ig_v[rows, :] = (cot_v[rows, :].astype(F32) + grad * slope_v[rows, :]).astype(BF)

    hidden(0)
    transpose(0)
    hidden(1)
    kg1_and_mixer(0, 2)
    core_send(0)
    hidden(2, 0, 2)
    y_send(0)
    hidden(2, 2, NR)
    kg1_and_mixer(2, 1)
    vectors()
    vec_step(0)
    loop(2, leave)
    z_send(0)
    loop(2, lambda i: leave(i + 2))
    kg02(0)
    core_send(1)
    vec_step(1)
    y_send(1)
    x_send(0)
    kg02(1)
    core_send(2)
    z_gather(0)
    y_send(2)
    vec_step(2)
    z_send(1)
    kg02(2)
    core_send(LAST)
    z_send(2)
    y_gather(0)
    last_xy()
    x_send(1)
    x_send(2)
    z_gather(1)
    grad_in(0)
    core_gather(0)
    z_gather(2)
    last_z()
    vec_step(3)
    grad_in(1)
    y_gather(1)
    last_z_gather()
    y_gather(2)
    grad_in(2)
    last_xy_gather()
    grad_in(3)
    core_gather(1)
    core_gather(2)
    vec_step(4)
    core_gather(LAST)
    for s in range(len(SEGS)):
        finish(s)

    for d, ref in ((0, t0_v), (1, t2_v), (2, t0_v), (3, t2_v)):
        pltpu.make_async_remote_copy(
            src_ref=ref, dst_ref=ref, send_sem=halo_send.at[d], recv_sem=tap_recv.at[0, 0, 0],
            device_id=sibling, device_id_type=MESH,
        ).wait_send()
    for stage in range(len(vec_stages)):
        vec_all(stage).wait_send()
    for s in range(len(SEGS)):
        for stage in range(7):
            if s != LAST or stage != X:
                total(s, stage, bulk(s, stage)).wait_send()


def finish_kernel(
    factor, lo_v, ig_v, gg_v, vec_in, lo_out, ig_out, kg_out, mg_out, offset_out, biases_out, kg_v, mg_v, sem
):
    stores = [
        pltpu.make_async_copy(lo_v, lo_out, sem.at[0]),
        pltpu.make_async_copy(ig_v, ig_out, sem.at[1]),
        pltpu.make_async_copy(mg_v, mg_out, sem.at[2]),
    ]
    stores += [pltpu.make_async_copy(kg_v.at[k], kg_out.at[k], sem.at[3 + k]) for k in range(3)]

    def spread(k, start):
        for c in range(NC):
            def body(i, carry, c=c):
                rows = pl.ds(pl.multiple_of(i * 128, 128), 128)
                source = pl.ds(pl.multiple_of(start + c * PAIR + i * 128, 128), 128)
                kg_v[k, rows, c * W:(c + 1) * W] = gg_v[source, :].astype(F32) * factor
                return carry

            lax.fori_loop(0, C // 128, body, 0)
        stores[3 + k].start()

    spread(1, KG1_AT)
    spread(0, KG02_AT)
    spread(2, KG02_AT + C)
    for c in range(H // W):
        for j in range(C // W):
            at = MG_AT + c * PAIR + j * W
            mg_v[c * W:(c + 1) * W, j * W:(j + 1) * W] = gg_v[at:at + W, :].astype(F32) * factor
    for copy in stores[2::-1]:
        copy.start()
    vec = vec_in[...] * factor
    biases_out[...] = vec[:C // W].reshape(C)
    offset_out[...] = vec[C // W:(C + H) // W].reshape(H)
    for copy in stores:
        copy.wait()


def local(features, kernel, offsets, mixer, biases, cotangent):
    length = features.shape[0] * lax.axis_size("seq") * lax.axis_size("sub")
    factor = 1.0 / math.sqrt(length)
    hbm_spec = pl.BlockSpec(memory_space=pltpu.HBM)
    vmem_spec = pl.BlockSpec(memory_space=pltpu.VMEM)
    n = len(SEGS)
    vm = pltpu.VMEM
    dma = pltpu.SemaphoreType.DMA
    lo, ig, gg, vec = pl.pallas_call(
        main_kernel,
        out_shape=(
            jax.ShapeDtypeStruct((ROWS, C), BF),
            jax.ShapeDtypeStruct((ROWS, C), BF),
            jax.ShapeDtypeStruct((TOTAL, W), BF),
            jax.ShapeDtypeStruct((VEC, W), F32),
        ),
        in_specs=[hbm_spec] * 6,
        out_specs=(vmem_spec,) * 4,
        scratch_shapes=[
            vm((ROWS, C), BF), vm((ROWS, C), BF), vm((NC, C, 2 * W), BF), vm((C, H), BF), vm((H, C), BF), vm((H,), F32), vm((C,), F32),
            vm((ROWS, C), BF), vm((C, ROWS), BF), vm((ROWS, C), F32), vm((ROWS, H), F32), vm((ROWS, H), F32),
            vm((NC, ROWS, W), BF), vm((NC, ROWS, W), BF), vm((NC, ROWS, W), BF), vm((NC, ROWS, W), BF),
            vm((ROWS, H), BF), vm((H, ROWS), BF), vm((ROWS, H), BF), vm((NC, ROWS, 2 * W), BF),
            vm((TOTAL, W), F32),
            vm((TOTAL // 2, W), BF), vm((TOTAL // 2, W), BF), vm((TOTAL // 2, W), BF), vm((TOTAL // 8 * 3, W), BF),
            vm((TOTAL // 8, W), BF), vm((TOTAL // 64 * 7, W), BF), vm((TOTAL // 64, W), BF),
            vm((TOTAL // 64 * 4, W), BF),
            vm((NP, SHARE, W), BF), vm((NP - 1, SHARE, W), BF), vm((NZ, SLICE, W), F32), vm((NZ, SLICE, W), BF),
            vm((NZ - 1, SLICE, W), BF), vm((NZ, SLICE, W), BF),
            vm((4, VEC, W), F32), vm((2, VEC, W), F32), vm((NY, VEC, W), F32), vm((NZ, VEC, W), F32),
            vm((NX, VEC, W), F32),
            dma((NR,)), dma((2 * NC + 5,)), dma((4,)), dma((2, NC, NR)), dma((2, NC, NR)),
            dma((n, 7)), dma((n, 7)), dma((4,)), dma((4,)),
        ],
        compiler_params=pltpu.CompilerParams(
            collective_id=0, has_side_effects=True, vmem_limit_bytes=46 * 2**20
        ),
        cost_estimate=pl.CostEstimate(flops=8_000_000_000, bytes_accessed=16_000_000, transcendentals=1_200_000),
        name="block",
    )(*[pltpu.with_memory_space_constraint(v, pltpu.HBM) for v in (features, kernel, offsets, mixer, biases, cotangent)])
    layer_output, input_grad, kernel_grad, mixer_grad, offset_grad, biases_grad = pl.pallas_call(
        lambda *refs: finish_kernel(factor, *refs),
        out_shape=(
            jax.ShapeDtypeStruct((ROWS, C), BF),
            jax.ShapeDtypeStruct((ROWS, C), BF),
            jax.ShapeDtypeStruct((3, C, H), F32),
            jax.ShapeDtypeStruct((H, C), F32),
            jax.ShapeDtypeStruct((H,), F32),
            jax.ShapeDtypeStruct((C,), F32),
        ),
        in_specs=[vmem_spec] * 4,
        out_specs=(hbm_spec,) * 4 + (vmem_spec,) * 2,
        scratch_shapes=[vm((3, C, H), F32), vm((H, C), F32), dma((6,))],
        compiler_params=pltpu.CompilerParams(vmem_limit_bytes=12 * 2**20),
        name="finish",
    )(lo, ig, gg, vec)
    return (layer_output, input_grad, kernel_grad, offset_grad, mixer_grad, biases_grad)


def solution(mesh):
    placed = (P(("seq", "sub"), None), P(), P(), P(), P(), P(("seq", "sub"), None))
    return jax.shard_map(
        local,
        mesh=mesh,
        in_specs=placed,
        out_specs=(P(("seq", "sub"), None), P(("seq", "sub"), None), P(), P(), P(), P()),
        check_vma=False,
    )
```

```python
import math

import jax
import jax.numpy as jnp
from jax import lax
from jax.experimental import pallas as pl
from jax.experimental.pallas import tpu as pltpu
from jax.sharding import PartitionSpec as P

MESH = pl.DeviceIdType.MESH
BF = jnp.bfloat16
F32 = jnp.float32

DILATION_STEP = 8192
C = 768
H = 384
ROWS = 1024
W = 128
NC = H // W
NR = 4
RB = ROWS // NR

NX, NY, NZ = 4, 4, 8

PAIR = 2 * C
KG1_AT, MG_AT, KG02_AT = 0, C, NC * PAIR
TOTAL = 2 * NC * PAIR
SEGS = ((0, 3072), (3072, 3072), (6144, 1536), (7680, 1536))
LATE = 2
NP = NX * NY
SHARE = SEGS[LATE][1] // (2 * NP)
VEC = 16

T_SCALE = 0.3
TAIL = (
    0.11962923731872051,
    0.12075488221323095,
    0.0999078411835699,
    0.12857978094297895,
    -0.05371691656802647,
    0.20638841535029362,
    -0.1572225638776185,
    0.03567924927328374,
)


def gelu_and_slope(v):
    u = jnp.abs(v)
    t = 1.0 / (1.0 + T_SCALE * u)
    poly = TAIL[-1]
    for coef in TAIL[-2::-1]:
        poly = poly * t + coef
    bell = jnp.exp(-0.5 * u * u)
    tail = poly * t * bell
    cdf = jnp.where(v >= 0.0, 1.0 - tail, tail)
    return v * cdf, cdf + v * bell * (1.0 / math.sqrt(2.0 * math.pi))


def nn(a, b):
    return jnp.dot(a, b, preferred_element_type=F32)


def nt(a, b):
    return lax.dot_general(a, b, (((1,), (1,)), ((), ())), preferred_element_type=F32)


def position():
    seq, sub = lax.axis_index("seq"), lax.axis_index("sub")
    z, x = lax.div(seq, 2 * NX), lax.rem(lax.div(seq, 2), NX)
    y = lax.div(sub, 2) * 2 + lax.rem(seq, 2)
    return seq, sub, x, y, z, lax.rem(sub, 2)


def device(x, y, z, core):
    return (z * (2 * NX) + x * 2 + lax.rem(y, 2), lax.div(y, 2) * 2 + core)


def main_kernel(
    f_hbm, k_hbm, off_hbm, mix_hbm, bias_hbm, cot_hbm,
    lo_v, ig_v, gg_v, vec_ref,
    f_v, cot_v, kw_v, k1_v, mix_v, off_v, bias_v,
    act_v, actt_v, slope_v, pre_v, hg_v,
    t0_v, t2_v, te_v, tl_v, hid_v, hidt_v, pg_v, pg02_v,
    g_v, sbc, rbc, sby, rby, sbz, rbz, sbx, rbx,
    late_s, late_r, late_zs, late_z,
    vs, vc, vy, vz, vx,
    f_sem, in_sem, halo_send, tap_recv, pg_recv, seg_send, seg_recv, vec_send, vec_recv,
):
    seq, sub, x, y, z, core = position()
    nseq = 2 * NX * NZ
    ahead = (lax.rem(seq + 2, nseq), sub)
    behind = (lax.rem(seq + nseq - 2, nseq), sub)

    def y_peer(d):
        return device(x, lax.rem(y + d, NY), z, core)

    def z_peer(d):
        return device(x, y, lax.rem(z + d, NZ), core)

    def x_peer(d):
        return device(lax.rem(x + d, NX), y, z, core)

    def xy_at(d):
        return lax.rem(x * NY + y + d, NP)

    def xy_peer(d):
        return device(lax.div(xy_at(d), NY), lax.rem(xy_at(d), NY), z, core)

    sibling = device(x, y, z, 1 - core)

    barrier = pltpu.get_barrier_semaphore()

    def greet(to):
        pl.semaphore_signal(barrier, inc=1, device_id=to, device_id_type=MESH)

    def greet_loop(n, peer):
        def body(d, carry):
            greet(peer(d))
            return carry

        lax.fori_loop(1, n, body, 0)

    def f_copy(r):
        rows = pl.ds(pl.multiple_of(r * RB, RB), RB)
        return pltpu.make_async_copy(f_hbm.at[rows], f_v.at[rows], f_sem.at[r])

    ins = []
    for c in range(NC):
        lanes = pl.ds(c * W, W)
        ins.append((k_hbm.at[0, :, lanes], kw_v.at[c, :, pl.ds(0, W)]))
        ins.append((k_hbm.at[2, :, lanes], kw_v.at[c, :, pl.ds(W, W)]))
    ins.append((k_hbm.at[1], k1_v))
    ins.append((mix_hbm, mix_v))
    ins.append((cot_hbm, cot_v))
    ins.append((off_hbm, off_v))
    ins.append((bias_hbm, bias_v))
    ins = [pltpu.make_async_copy(s, d, in_sem.at[i]) for i, (s, d) in enumerate(ins)]
    f_copy(0).start()
    ins[0].start()
    ins[1].start()
    for r in range(1, NR):
        f_copy(r).start()
    for copy in ins[2:]:
        copy.start()

    greet(sibling)
    greet(ahead)
    greet(behind)
    greet_loop(NP, xy_peer)
    greet_loop(NZ, z_peer)

    def loop(n, body):
        def step(i, carry):
            body(i)
            return carry

        lax.fori_loop(0, n, step, 0)

    def rows_at(base, i, n):
        return pl.ds(pl.multiple_of(base + i * n, n), n)

    def activate(r):
        def body(i):
            rows = pl.ds(pl.multiple_of(r * RB + i * 16, 16), 16)
            gelu, slope = gelu_and_slope(f_v[rows, :].astype(F32))
            act_v[rows, :] = gelu.astype(BF)
            slope_v[rows, :] = slope

        loop(RB // 16, body)

    def tap_copies(c, r):
        rows = pl.ds(pl.multiple_of(r * RB, RB), RB)
        return (
            pltpu.make_async_remote_copy(
                src_ref=t0_v.at[c, rows], dst_ref=te_v.at[c, rows],
                send_sem=halo_send.at[0], recv_sem=tap_recv.at[0, c, r],
                device_id=ahead, device_id_type=MESH,
            ),
            pltpu.make_async_remote_copy(
                src_ref=t2_v.at[c, rows], dst_ref=tl_v.at[c, rows],
                send_sem=halo_send.at[1], recv_sem=tap_recv.at[1, c, r],
                device_id=behind, device_id_type=MESH,
            ),
        )

    def taps(c, r):
        rows = pl.ds(pl.multiple_of(r * RB, RB), RB)
        both = nn(act_v[rows, :], kw_v[c]).astype(BF)
        t0_v[c, rows, :] = both[:, :W]
        t2_v[c, rows, :] = both[:, W:]

    def send_taps(c, r):
        for copy in tap_copies(c, r):
            copy.start()

    with jax.named_scope("start"):
        f_copy(0).wait()
        activate(0)
        ins[0].wait()
        ins[1].wait()
        taps(0, 0)
    with jax.named_scope("greeted"):
        pl.semaphore_wait(barrier, 1 + 2 + (NP - 1) + (NZ - 1))
    send_taps(0, 0)

    def first(i):
        r = i + 1
        f_copy(r).wait()
        activate(r)
        taps(0, r)
        send_taps(0, r)

    with jax.named_scope("first"):
        loop(NR - 1, first)
    for c in range(1, NC):
        ins[2 * c].wait()
        ins[2 * c + 1].wait()

        def more(r, c=c):
            taps(c, r)
            send_taps(c, r)

        with jax.named_scope("more_taps"):
            loop(NR, more)

    for copy in ins[2 * NC:]:
        copy.wait()

    def own(r):
        rows = pl.ds(pl.multiple_of(r * RB, RB), RB)
        pre_v[rows, :] = nn(act_v[rows, :], k1_v[...]) + off_v[...].reshape(1, H)
        hg_v[rows, :] = nt(cot_v[rows, :], mix_v[...])

    with jax.named_scope("own"):
        loop(NR, own)

    def pg_copies(c, r):
        rows = pl.ds(pl.multiple_of(r * RB, RB), RB)
        src = pg_v.at[rows, pl.ds(c * W, W)]
        return (
            pltpu.make_async_remote_copy(
                src_ref=src, dst_ref=pg02_v.at[c, rows, pl.ds(0, W)],
                send_sem=halo_send.at[2], recv_sem=pg_recv.at[0, c, r],
                device_id=behind, device_id_type=MESH,
            ),
            pltpu.make_async_remote_copy(
                src_ref=src, dst_ref=pg02_v.at[c, rows, pl.ds(W, W)],
                send_sem=halo_send.at[3], recv_sem=pg_recv.at[1, c, r],
                device_id=ahead, device_id_type=MESH,
            ),
        )

    def hidden(c, first=0, last=NR):
        lanes = slice(c * W, (c + 1) * W)

        def block(r):
            for copy in tap_copies(c, r):
                copy.wait_recv()

            def body(i):
                rows = pl.ds(pl.multiple_of(r * RB + i * 64, 64), 64)
                pre = pre_v[rows, lanes] + te_v[c, rows, :].astype(F32) + tl_v[c, rows, :].astype(F32)
                gelu, slope = gelu_and_slope(pre)
                hid_v[rows, lanes] = gelu.astype(BF)
                pg_v[rows, lanes] = (hg_v[rows, lanes] * slope).astype(BF)

            loop(RB // 64, body)
            for copy in pg_copies(c, r):
                copy.start()

        loop(last - first, lambda i: block(first + i))

    CORE, Y, Z, X, GZ, GY, GC = range(7)

    def ds(base, n):
        return pl.ds(pl.multiple_of(base, 16), n)

    def sizes(s):
        at, n = SEGS[s]
        return at, n // 2, n // 8, n // 64

    def own_half(s):
        at, half, *_ = sizes(s)
        return at + core * half

    def part_at(s, ty, tz):
        return (ty * NZ + tz if s == 0 else tz * NY + ty) * sizes(s)[3]

    def send(s, stage, src, dst, to):
        pltpu.make_async_remote_copy(
            src_ref=src, dst_ref=dst, send_sem=seg_send.at[s, stage], recv_sem=seg_recv.at[s, stage],
            device_id=to, device_id_type=MESH,
        ).start()

    def each(n, body):
        def step(d, carry):
            body(d)
            return carry

        lax.fori_loop(1, n, step, 0)

    def bulk(s, stage):
        at, half, quarter, part = sizes(s)
        if stage in (CORE, GC):
            return rbc.at[pl.ds(at // 2, half)]
        if s >= LATE:
            return late_z.at[s - LATE, pl.ds(0, NZ - 1)] if stage == Z else late_r.at[s - LATE]
        if s == 1 and stage == GY:
            return rbc.at[pl.ds(at // 2, (NY - 1) * part)]
        if s == 1 and stage == GZ:
            return rbc.at[pl.ds(at // 2, (NZ - 1) * NY * part)]
        if stage in (Y, GY):
            return rby.at[pl.ds(at // 8 * 3, 3 * quarter)]
        if stage in (Z, GZ):
            return rbz.at[pl.ds(at // 64 * 7, 7 * part)]
        return rbx.at[pl.ds(at // 64 * 4, 3 * part)]

    def total(s, stage):
        ref = bulk(s, stage)
        return pltpu.make_async_remote_copy(
            src_ref=ref, dst_ref=ref, send_sem=seg_send.at[s, stage], recv_sem=seg_recv.at[s, stage],
            device_id=sibling, device_id_type=MESH,
        )

    def core_send(s):
        at, half, *_ = sizes(s)
        other = at + (1 - core) * half

        def body(i):
            sbc[pl.ds(pl.multiple_of(at // 2 + i * 128, 128), 128), :] = g_v[
                ds(other + i * 128, 128), :
            ].astype(BF)

        loop(half // 128, body)
        rows = pl.ds(at // 2, half)
        send(s, CORE, sbc.at[rows], rbc.at[rows], sibling)

    def y_send(s):
        at, half, quarter, part = sizes(s)
        total(s, CORE).wait_recv()

        def body(i):
            rows = ds(own_half(s) + i * 128, 128)
            got = pl.ds(pl.multiple_of(at // 2 + i * 128, 128), 128)
            summed = g_v[rows, :] + rbc[got, :].astype(F32)
            g_v[rows, :] = summed
            sby[got, :] = summed.astype(BF)

        loop(half // 128, body)
        if s == 0:
            each(NY, lambda d: send(
                s, Y, sby.at[ds(at // 2 + part_at(s, lax.rem(y + d, NY), 0), quarter)],
                rby.at[ds(at // 8 * 3 + (d - 1) * quarter, quarter)], y_peer(d),
            ))
        else:
            def blocks(i):
                d, tz = 1 + lax.div(i, NZ), lax.rem(i, NZ)
                send(
                    s, Y, sby.at[ds(at // 2 + part_at(s, lax.rem(y + d, NY), tz), part)],
                    rby.at[ds(at // 8 * 3 + (d - 1) * quarter + tz * part, part)], y_peer(d),
                )

            loop((NY - 1) * NZ, blocks)

    def z_send(s):
        at, half, quarter, part = sizes(s)
        total(s, Y).wait_recv()

        def body(i):
            rows = ds(own_half(s) + part_at(s, y, i), part)
            summed = g_v[rows, :]
            for d in range(NY - 1):
                summed = summed + rby[ds(at // 8 * 3 + d * quarter + i * part, part), :].astype(F32)
            g_v[rows, :] = summed
            sbz[ds(at // 8 + i * part, part), :] = summed.astype(BF)

        loop(NZ, body)
        each(NZ, lambda d: send(
            s, Z, sbz.at[ds(at // 8 + lax.rem(z + d, NZ) * part, part)],
            rbz.at[ds(at // 64 * 7 + (d - 1) * part, part)], z_peer(d),
        ))

    def x_send(s):
        at, half, quarter, part = sizes(s)
        total(s, Z).wait_recv()
        summed = g_v[ds(own_half(s) + part_at(s, y, z), part), :]
        for d in range(NZ - 1):
            summed = summed + rbz[ds(at // 64 * 7 + d * part, part), :].astype(F32)
        rows = ds(at // 64 * 4 + x * part, part)
        sbx[pl.ds(at // 64, part), :] = summed.astype(BF)
        rbx[rows, :] = summed.astype(BF)
        each(NX, lambda d: send(s, X, sbx.at[pl.ds(at // 64, part)], rbx.at[rows], x_peer(d)))

    def summed_over_x(s):
        at, half, quarter, part = sizes(s)
        total(s, X).wait_recv()
        summed = rbx[pl.ds(at // 64 * 4, part), :].astype(F32)
        for k in range(1, NX):
            summed = summed + rbx[pl.ds(at // 64 * 4 + k * part, part), :].astype(F32)
        rows = ds(own_half(s) + part_at(s, y, z), part)
        gg_v[rows, :] = summed.astype(BF)
        return gg_v.at[rows]

    def gather(s):
        ref = summed_over_x(s)
        if s == 0:
            each(NZ, lambda d: send(s, GZ, ref, ref, z_peer(d)))
        else:
            each(NY, lambda d: send(s, GY, ref, ref, y_peer(d)))

    def gather_more(s):
        at, half, quarter, part = sizes(s)
        if s == 0:
            total(s, GZ).wait_recv()
            ref = gg_v.at[ds(own_half(s) + part_at(s, y, 0), quarter)]
            each(NY, lambda d: send(s, GY, ref, ref, y_peer(d)))
        else:
            total(s, GY).wait_recv()
            ref = gg_v.at[ds(own_half(s) + part_at(s, 0, z), NY * part)]
            each(NZ, lambda d: send(s, GZ, ref, ref, z_peer(d)))

    def late_rows(s):
        return ds(own_half(s) + xy_at(0) * SHARE, SHARE)

    def xy_send(s):
        at, half, *_ = sizes(s)
        k = s - LATE
        total(s, CORE).wait_recv()

        def body(i):
            rows = ds(own_half(s) + i * SHARE, SHARE)
            summed = g_v[rows, :] + rbc[ds(at // 2 + i * SHARE, SHARE), :].astype(F32)
            g_v[rows, :] = summed
            late_s[k, i] = summed.astype(BF)

        loop(NP, body)
        each(NP, lambda d: send(s, Y, late_s.at[k, xy_at(d)], late_r.at[k, d - 1], xy_peer(d)))

    def z_all(s):
        k = s - LATE
        total(s, Y).wait_recv()
        summed = g_v[late_rows(s), :]
        for d in range(NP - 1):
            summed = summed + late_r[k, d].astype(F32)
        late_zs[k] = summed.astype(BF)
        late_z[k, z] = summed.astype(BF)
        each(NZ, lambda d: send(s, Z, late_zs.at[k], late_z.at[k, z], z_peer(d)))

    def xy_gather(s):
        k = s - LATE
        total(s, Z).wait_recv()
        summed = late_z[k, 0].astype(F32)
        for i in range(1, NZ):
            summed = summed + late_z[k, i].astype(F32)
        gg_v[late_rows(s), :] = summed.astype(BF)
        ref = gg_v.at[late_rows(s)]
        each(NP, lambda d: send(s, GY, ref, ref, xy_peer(d)))

    def core_gather(s):
        total(s, GZ if s == 1 else GY).wait_recv()
        ref = gg_v.at[ds(own_half(s), sizes(s)[1])]
        send(s, GC, ref, ref, sibling)

    def finish(s):
        total(s, GC).wait_recv()

    vec_stages = ((vc, 2, core, lambda d: sibling), (vy, NY, y, y_peer), (vz, NZ, z, z_peer), (vx, NX, x, x_peer))

    def vec_all(stage):
        ref, n, _, _ = vec_stages[stage]
        whole = ref.at[pl.ds(0, n - 1)]
        return pltpu.make_async_remote_copy(
            src_ref=whole, dst_ref=whole, send_sem=vec_send.at[stage], recv_sem=vec_recv.at[stage],
            device_id=sibling, device_id_type=MESH,
        )

    def vec_step(stage):
        if stage == 0:
            value = vs[0]
        else:
            vec_all(stage - 1).wait_recv()
            before, n, _, _ = vec_stages[stage - 1]
            value = before[0]
            for k in range(1, n):
                value = value + before[k]
        if stage == len(vec_stages):
            vec_ref[...] = value
            return
        ref, n, me, peer = vec_stages[stage]
        vs[stage] = value
        ref[me] = value

        def to(d, carry):
            pltpu.make_async_remote_copy(
                src_ref=vs.at[stage], dst_ref=ref.at[me],
                send_sem=vec_send.at[stage], recv_sem=vec_recv.at[stage],
                device_id=peer(d), device_id_type=MESH,
            ).start()
            return carry

        lax.fori_loop(1, n, to, 0)

    def transpose(r):
        for r in range(NR):
            rows = pl.ds(r * RB, RB)
            actt_v[:, rows] = act_v[rows, :].T

    def kg1_and_mixer(c, n):
        lanes = slice(c * W, (c + n) * W)
        for r in range(NR):
            rows = pl.ds(r * RB, RB)
            hidt_v[lanes, rows] = hid_v[rows, lanes].T

        def kg1(m):
            part = nn(actt_v[pl.ds(pl.multiple_of(m * 256, 256), 256), :], pg_v[:, lanes])
            for k in range(n):
                at = KG1_AT + (c + k) * PAIR + m * 256
                g_v[pl.ds(pl.multiple_of(at, 256), 256), :] = part[:, k * W:(k + 1) * W]

        loop(C // 256, kg1)
        for j in range(C // 256):
            part = nn(hidt_v[lanes, :], cot_v[:, j * 256:(j + 1) * 256])
            for i in range(n):
                for k in range(2):
                    at = MG_AT + (c + i) * PAIR + (j * 2 + k) * W
                    g_v[pl.ds(at, W), :] = part[i * W:(i + 1) * W, k * W:(k + 1) * W]

    def vectors():
        ones = jnp.ones((8, ROWS), BF)
        cot_sum = nn(ones, cot_v[...])
        pg_sum = nn(ones, pg_v[...])
        for j in range(C // W):
            vs[0, j:j + 1, :] = cot_sum[:1, j * W:(j + 1) * W]
        for j in range(H // W):
            vs[0, C // W + j:C // W + j + 1, :] = pg_sum[:1, j * W:(j + 1) * W]
        done = C // W + H // W
        vs[0, done:, :] = jnp.zeros((VEC - done, W), F32)

    def kg02(c):
        def wait(r):
            for copy in pg_copies(c, r):
                copy.wait_recv()

        loop(NR, wait)

        def block(m):
            part = nn(actt_v[pl.ds(pl.multiple_of(m * 256, 256), 256), :], pg02_v[c])
            at = KG02_AT + c * PAIR + m * 256
            g_v[pl.ds(pl.multiple_of(at, 256), 256), :] = part[:, :W]
            g_v[pl.ds(pl.multiple_of(at + C, 256), 256), :] = part[:, W:]

        loop(C // 256, block)

    def leave(r):
        rows = pl.ds(pl.multiple_of(r * RB, RB), RB)
        lo_v[rows, :] = (f_v[rows, :].astype(F32) + nn(hid_v[rows, :], mix_v[...]) + bias_v[...].reshape(1, C)).astype(BF)

    def grad_in(r):
        rows = pl.ds(pl.multiple_of(r * RB, RB), RB)
        grad = nt(pg_v[rows, :], k1_v[...])
        for c in range(NC):
            grad = grad + nt(pg02_v[c, rows, :], kw_v[c])
        ig_v[rows, :] = (cot_v[rows, :].astype(F32) + grad * slope_v[rows, :]).astype(BF)

    hidden(0)
    transpose(0)
    hidden(1)
    kg1_and_mixer(0, 2)
    core_send(0)
    hidden(2, 0, 2)
    y_send(0)
    hidden(2, 2, NR)
    kg1_and_mixer(2, 1)
    vectors()
    vec_step(0)
    loop(NR, leave)
    z_send(0)
    vec_step(1)
    kg02(0)
    core_send(1)
    vec_step(2)
    y_send(1)
    kg02(1)
    core_send(2)
    kg02(2)
    core_send(3)
    xy_send(2)
    z_send(1)
    xy_send(3)
    grad_in(0)
    x_send(0)
    grad_in(1)
    vec_step(3)
    z_all(2)
    gather(0)
    x_send(1)
    z_all(3)
    grad_in(2)
    gather(1)
    gather_more(0)
    xy_gather(2)
    gather_more(1)
    xy_gather(3)
    grad_in(3)
    vec_step(4)
    core_gather(0)
    core_gather(2)
    core_gather(1)
    core_gather(3)
    for s in range(len(SEGS)):
        finish(s)

    for d, ref in ((0, t0_v), (1, t2_v), (2, t0_v), (3, t2_v)):
        pltpu.make_async_remote_copy(
            src_ref=ref, dst_ref=ref, send_sem=halo_send.at[d], recv_sem=tap_recv.at[0, 0, 0],
            device_id=sibling, device_id_type=MESH,
        ).wait_send()
    for stage in range(len(vec_stages)):
        vec_all(stage).wait_send()
    for s in range(len(SEGS)):
        for stage in range(7):
            if s < LATE or stage not in (X, GZ):
                total(s, stage).wait_send()


def finish_kernel(
    factor, lo_v, ig_v, gg_v, vec_in, lo_out, ig_out, kg_out, mg_out, offset_out, biases_out, kg_v, mg_v, sem
):
    stores = [
        pltpu.make_async_copy(lo_v, lo_out, sem.at[0]),
        pltpu.make_async_copy(ig_v, ig_out, sem.at[1]),
        pltpu.make_async_copy(mg_v, mg_out, sem.at[2]),
    ]
    stores += [pltpu.make_async_copy(kg_v.at[k], kg_out.at[k], sem.at[3 + k]) for k in range(3)]

    def spread(k, start):
        for c in range(NC):
            def body(i, carry, c=c):
                rows = pl.ds(pl.multiple_of(i * 128, 128), 128)
                source = pl.ds(pl.multiple_of(start + c * PAIR + i * 128, 128), 128)
                kg_v[k, rows, c * W:(c + 1) * W] = gg_v[source, :].astype(F32) * factor
                return carry

            lax.fori_loop(0, C // 128, body, 0)
        stores[3 + k].start()

    spread(1, KG1_AT)
    spread(0, KG02_AT)
    spread(2, KG02_AT + C)
    for c in range(H // W):
        for j in range(C // W):
            at = MG_AT + c * PAIR + j * W
            mg_v[c * W:(c + 1) * W, j * W:(j + 1) * W] = gg_v[at:at + W, :].astype(F32) * factor
    for copy in stores[2::-1]:
        copy.start()
    vec = vec_in[...] * factor
    biases_out[...] = vec[:C // W].reshape(C)
    offset_out[...] = vec[C // W:(C + H) // W].reshape(H)
    for copy in stores:
        copy.wait()


def local(features, kernel, offsets, mixer, biases, cotangent):
    length = features.shape[0] * lax.axis_size("seq") * lax.axis_size("sub")
    factor = 1.0 / math.sqrt(length)
    hbm_spec = pl.BlockSpec(memory_space=pltpu.HBM)
    vmem_spec = pl.BlockSpec(memory_space=pltpu.VMEM)
    n = len(SEGS)
    vm = pltpu.VMEM
    dma = pltpu.SemaphoreType.DMA
    lo, ig, gg, vec = pl.pallas_call(
        main_kernel,
        out_shape=(
            jax.ShapeDtypeStruct((ROWS, C), BF),
            jax.ShapeDtypeStruct((ROWS, C), BF),
            jax.ShapeDtypeStruct((TOTAL, W), BF),
            jax.ShapeDtypeStruct((VEC, W), F32),
        ),
        in_specs=[hbm_spec] * 6,
        out_specs=(vmem_spec,) * 4,
        scratch_shapes=[
            vm((ROWS, C), BF), vm((ROWS, C), BF), vm((NC, C, 2 * W), BF), vm((C, H), BF), vm((H, C), BF), vm((H,), F32), vm((C,), F32),
            vm((ROWS, C), BF), vm((C, ROWS), BF), vm((ROWS, C), F32), vm((ROWS, H), F32), vm((ROWS, H), F32),
            vm((NC, ROWS, W), BF), vm((NC, ROWS, W), BF), vm((NC, ROWS, W), BF), vm((NC, ROWS, W), BF),
            vm((ROWS, H), BF), vm((H, ROWS), BF), vm((ROWS, H), BF), vm((NC, ROWS, 2 * W), BF),
            vm((TOTAL, W), F32),
            vm((TOTAL // 2, W), BF), vm((TOTAL // 2, W), BF), vm((TOTAL // 2, W), BF), vm((TOTAL // 8 * 3, W), BF),
            vm((TOTAL // 8, W), BF), vm((TOTAL // 64 * 7, W), BF), vm((TOTAL // 64, W), BF),
            vm((TOTAL // 64 * 4, W), BF),
            vm((2, NP, SHARE, W), BF), vm((2, NP - 1, SHARE, W), BF), vm((2, SHARE, W), BF), vm((2, NZ, SHARE, W), BF),
            vm((4, VEC, W), F32), vm((2, VEC, W), F32), vm((NY, VEC, W), F32), vm((NZ, VEC, W), F32),
            vm((NX, VEC, W), F32),
            dma((NR,)), dma((2 * NC + 5,)), dma((4,)), dma((2, NC, NR)), dma((2, NC, NR)),
            dma((n, 7)), dma((n, 7)), dma((4,)), dma((4,)),
        ],
        compiler_params=pltpu.CompilerParams(
            collective_id=0, has_side_effects=True, vmem_limit_bytes=46 * 2**20
        ),
        cost_estimate=pl.CostEstimate(flops=8_000_000_000, bytes_accessed=16_000_000, transcendentals=1_200_000),
        name="block",
    )(*[pltpu.with_memory_space_constraint(v, pltpu.HBM) for v in (features, kernel, offsets, mixer, biases, cotangent)])
    layer_output, input_grad, kernel_grad, mixer_grad, offset_grad, biases_grad = pl.pallas_call(
        lambda *refs: finish_kernel(factor, *refs),
        out_shape=(
            jax.ShapeDtypeStruct((ROWS, C), BF),
            jax.ShapeDtypeStruct((ROWS, C), BF),
            jax.ShapeDtypeStruct((3, C, H), F32),
            jax.ShapeDtypeStruct((H, C), F32),
            jax.ShapeDtypeStruct((H,), F32),
            jax.ShapeDtypeStruct((C,), F32),
        ),
        in_specs=[vmem_spec] * 4,
        out_specs=(hbm_spec,) * 4 + (vmem_spec,) * 2,
        scratch_shapes=[vm((3, C, H), F32), vm((H, C), F32), dma((6,))],
        compiler_params=pltpu.CompilerParams(vmem_limit_bytes=12 * 2**20),
        name="finish",
    )(lo, ig, gg, vec)
    return (layer_output, input_grad, kernel_grad, offset_grad, mixer_grad, biases_grad)


def solution(mesh):
    placed = (P(("seq", "sub"), None), P(), P(), P(), P(), P(("seq", "sub"), None))
    return jax.shard_map(
        local,
        mesh=mesh,
        in_specs=placed,
        out_specs=(P(("seq", "sub"), None), P(("seq", "sub"), None), P(), P(), P(), P()),
        check_vma=False,
    )
```

```python
import math

import jax
import jax.numpy as jnp
from jax import lax
from jax.experimental import pallas as pl
from jax.experimental.pallas import tpu as pltpu
from jax.sharding import PartitionSpec as P

MESH = pl.DeviceIdType.MESH
BF = jnp.bfloat16
F32 = jnp.float32

DILATION_STEP = 8192
C = 768
H = 384
ROWS = 1024
W = 128
NC = H // W
NR = 4
RB = ROWS // NR
NB = ROWS // 256

NX, NY, NZ = 4, 4, 8

PAIR = 2 * C
KG1_AT, MG_AT, KG02_AT = 0, C, NC * PAIR
TOTAL = 2 * NC * PAIR
SEGS = ((0, 3072), (3072, 3072), (6144, 1536), (7680, 1536))
LATE = 2
NP = NX * NY
SHARE = SEGS[LATE][1] // (2 * NP)
VEC = 16

T_SCALE = 0.3
TAIL = (
    0.11962923731872051,
    0.12075488221323095,
    0.0999078411835699,
    0.12857978094297895,
    -0.05371691656802647,
    0.20638841535029362,
    -0.1572225638776185,
    0.03567924927328374,
)


def gelu_and_slope(v):
    u = jnp.abs(v)
    t = 1.0 / (1.0 + T_SCALE * u)
    poly = TAIL[-1]
    for coef in TAIL[-2::-1]:
        poly = poly * t + coef
    bell = jnp.exp(-0.5 * u * u)
    tail = poly * t * bell
    cdf = jnp.where(v >= 0.0, 1.0 - tail, tail)
    return v * cdf, cdf + v * bell * (1.0 / math.sqrt(2.0 * math.pi))


def nn(a, b):
    return jnp.dot(a, b, preferred_element_type=F32)


def nt(a, b):
    return lax.dot_general(a, b, (((1,), (1,)), ((), ())), preferred_element_type=F32)


def position():
    seq, sub = lax.axis_index("seq"), lax.axis_index("sub")
    z, x = lax.div(seq, 2 * NX), lax.rem(lax.div(seq, 2), NX)
    y = lax.div(sub, 2) * 2 + lax.rem(seq, 2)
    return seq, sub, x, y, z, lax.rem(sub, 2)


def device(x, y, z, core):
    return (z * (2 * NX) + x * 2 + lax.rem(y, 2), lax.div(y, 2) * 2 + core)


def main_kernel(
    f_hbm, k_hbm, off_hbm, mix_hbm, bias_hbm, cot_hbm,
    lo_v, ig_v, gg_v, vec_ref,
    f_v, cot_v, kw_v, k1_v, mix_v, off_v, bias_v,
    act_v, actt_v, slope_v, grad_v, pre_v, hg_v,
    t0_v, t2_v, te_v, tl_v, hid_v, hidt_v, pg_v, pg02_v,
    g_v, sbc, rbc, sby, rby, sbz, rbz, sbx, rbx,
    late_s, late_r, late_zs, late_z,
    vs, vc, vy, vz, vx,
    f_sem, in_sem, halo_send, tap_recv, pg_recv, seg_send, seg_recv, vec_send, vec_recv,
):
    seq, sub, x, y, z, core = position()
    nseq = 2 * NX * NZ
    ahead = (lax.rem(seq + 2, nseq), sub)
    behind = (lax.rem(seq + nseq - 2, nseq), sub)

    def y_peer(d):
        return device(x, lax.rem(y + d, NY), z, core)

    def z_peer(d):
        return device(x, y, lax.rem(z + d, NZ), core)

    def x_peer(d):
        return device(lax.rem(x + d, NX), y, z, core)

    def xy_at(d):
        return lax.rem(x * NY + y + d, NP)

    def xy_peer(d):
        return device(lax.div(xy_at(d), NY), lax.rem(xy_at(d), NY), z, core)

    sibling = device(x, y, z, 1 - core)

    barrier = pltpu.get_barrier_semaphore()

    def greet(to):
        pl.semaphore_signal(barrier, inc=1, device_id=to, device_id_type=MESH)

    def greet_loop(n, peer):
        def body(d, carry):
            greet(peer(d))
            return carry

        lax.fori_loop(1, n, body, 0)

    def f_copy(r):
        rows = pl.ds(pl.multiple_of(r * RB, RB), RB)
        return pltpu.make_async_copy(f_hbm.at[rows], f_v.at[rows], f_sem.at[r])

    ins = []
    for c in range(NC):
        lanes = pl.ds(c * W, W)
        ins.append((k_hbm.at[0, :, lanes], kw_v.at[c, :, pl.ds(0, W)]))
        ins.append((k_hbm.at[2, :, lanes], kw_v.at[c, :, pl.ds(W, W)]))
    ins.append((k_hbm.at[1], k1_v))
    ins.append((mix_hbm, mix_v))
    ins.append((cot_hbm, cot_v))
    ins.append((off_hbm, off_v))
    ins.append((bias_hbm, bias_v))
    ins = [pltpu.make_async_copy(s, d, in_sem.at[i]) for i, (s, d) in enumerate(ins)]
    f_copy(0).start()
    ins[0].start()
    ins[1].start()
    for r in range(1, 3):
        f_copy(r).start()
    ins[2].start()
    ins[3].start()
    for r in range(3, NR):
        f_copy(r).start()
    for copy in ins[4:]:
        copy.start()

    greet(sibling)
    greet(ahead)
    greet(behind)
    greet_loop(NP, xy_peer)
    greet_loop(NZ, z_peer)

    def loop(n, body):
        def step(i, carry):
            body(i)
            return carry

        lax.fori_loop(0, n, step, 0)

    def rows_at(base, i, n):
        return pl.ds(pl.multiple_of(base + i * n, n), n)

    def activate(r):
        def body(i):
            rows = pl.ds(pl.multiple_of(r * RB + i * 16, 16), 16)
            gelu, slope = gelu_and_slope(f_v[rows, :].astype(F32))
            act_v[rows, :] = gelu.astype(BF)
            slope_v[rows, :] = slope

        loop(RB // 16, body)

    def tap_copies(c, r):
        rows = pl.ds(pl.multiple_of(r * RB, RB), RB)
        return (
            pltpu.make_async_remote_copy(
                src_ref=t0_v.at[c, rows], dst_ref=te_v.at[c, rows],
                send_sem=halo_send.at[0], recv_sem=tap_recv.at[0, c, r],
                device_id=ahead, device_id_type=MESH,
            ),
            pltpu.make_async_remote_copy(
                src_ref=t2_v.at[c, rows], dst_ref=tl_v.at[c, rows],
                send_sem=halo_send.at[1], recv_sem=tap_recv.at[1, c, r],
                device_id=behind, device_id_type=MESH,
            ),
        )

    def taps(c, r):
        rows = pl.ds(pl.multiple_of(r * RB, RB), RB)
        both = nn(act_v[rows, :], kw_v[c]).astype(BF)
        t0_v[c, rows, :] = both[:, :W]
        t2_v[c, rows, :] = both[:, W:]

    def send_taps(c, r):
        for copy in tap_copies(c, r):
            copy.start()

    def taps_of_two(r):
        for c in range(2):
            taps(c, r)
        for c in range(2):
            send_taps(c, r)

    f_copy(0).wait()
    activate(0)
    for copy in ins[:4]:
        copy.wait()
    taps(0, 0)
    pl.semaphore_wait(barrier, 1 + 2 + (NP - 1) + (NZ - 1))
    send_taps(0, 0)
    taps(1, 0)
    send_taps(1, 0)

    def first(i):
        r = i + 1
        f_copy(r).wait()
        activate(r)
        taps_of_two(r)

    loop(NR - 1, first)
    for copy in ins[4:6]:
        copy.wait()

    def third(r):
        taps(2, r)
        send_taps(2, r)

    loop(NR, third)
    for copy in ins[2 * NC:]:
        copy.wait()

    def own(r):
        rows = pl.ds(pl.multiple_of(r * 256, 256), 256)
        pre_v[rows, :] = nn(act_v[rows, :], k1_v[...]) + off_v[...].reshape(1, H)
        hg_v[rows, :] = nt(cot_v[rows, :], mix_v[...])

    with jax.named_scope("own"):
        loop(NB, own)

    def pg_copies(c, r):
        rows = pl.ds(pl.multiple_of(r * RB, RB), RB)
        src = pg_v.at[rows, pl.ds(c * W, W)]
        return (
            pltpu.make_async_remote_copy(
                src_ref=src, dst_ref=pg02_v.at[c, rows, pl.ds(0, W)],
                send_sem=halo_send.at[2], recv_sem=pg_recv.at[0, c, r],
                device_id=behind, device_id_type=MESH,
            ),
            pltpu.make_async_remote_copy(
                src_ref=src, dst_ref=pg02_v.at[c, rows, pl.ds(W, W)],
                send_sem=halo_send.at[3], recv_sem=pg_recv.at[1, c, r],
                device_id=ahead, device_id_type=MESH,
            ),
        )

    def hidden(c, first=0, last=NR):
        lanes = slice(c * W, (c + 1) * W)

        def block(r):
            for copy in tap_copies(c, r):
                copy.wait_recv()

            def body(i):
                rows = pl.ds(pl.multiple_of(r * RB + i * 64, 64), 64)
                pre = pre_v[rows, lanes] + te_v[c, rows, :].astype(F32) + tl_v[c, rows, :].astype(F32)
                gelu, slope = gelu_and_slope(pre)
                hid_v[rows, lanes] = gelu.astype(BF)
                pg_v[rows, lanes] = (hg_v[rows, lanes] * slope).astype(BF)

            loop(RB // 64, body)
            for copy in pg_copies(c, r):
                copy.start()

        loop(last - first, lambda i: block(first + i))

    CORE, Y, Z, X, GZ, GY, GC = range(7)

    def ds(base, n):
        return pl.ds(pl.multiple_of(base, 16), n)

    def sizes(s):
        at, n = SEGS[s]
        return at, n // 2, n // 8, n // 64

    def own_half(s):
        at, half, *_ = sizes(s)
        return at + core * half

    def part_at(s, ty, tz):
        return (ty * NZ + tz if s == 0 else tz * NY + ty) * sizes(s)[3]

    def send(s, stage, src, dst, to):
        pltpu.make_async_remote_copy(
            src_ref=src, dst_ref=dst, send_sem=seg_send.at[s, stage], recv_sem=seg_recv.at[s, stage],
            device_id=to, device_id_type=MESH,
        ).start()

    def each(n, body):
        def step(d, carry):
            body(d)
            return carry

        lax.fori_loop(1, n, step, 0)

    def bulk(s, stage):
        at, half, quarter, part = sizes(s)
        if stage in (CORE, GC):
            return rbc.at[pl.ds(at // 2, half)]
        if s >= LATE:
            return late_z.at[s - LATE, pl.ds(0, NZ - 1)] if stage == Z else late_r.at[s - LATE]
        if s == 1 and stage == GY:
            return rbc.at[pl.ds(at // 2, (NY - 1) * part)]
        if s == 1 and stage == GZ:
            return rbc.at[pl.ds(at // 2, (NZ - 1) * NY * part)]
        if stage in (Y, GY):
            return rby.at[pl.ds(at // 8 * 3, 3 * quarter)]
        if stage in (Z, GZ):
            return rbz.at[pl.ds(at // 64 * 7, 7 * part)]
        return rbx.at[pl.ds(at // 64 * 4, 3 * part)]

    def total(s, stage):
        ref = bulk(s, stage)
        return pltpu.make_async_remote_copy(
            src_ref=ref, dst_ref=ref, send_sem=seg_send.at[s, stage], recv_sem=seg_recv.at[s, stage],
            device_id=sibling, device_id_type=MESH,
        )

    def core_send(s):
        at, half, *_ = sizes(s)
        other = at + (1 - core) * half

        def body(i):
            sbc[pl.ds(pl.multiple_of(at // 2 + i * 128, 128), 128), :] = g_v[
                ds(other + i * 128, 128), :
            ].astype(BF)

        if s < LATE:
            loop(half // 128, body)
        rows = pl.ds(at // 2, half)
        send(s, CORE, sbc.at[rows], rbc.at[rows], sibling)

    def y_send(s):
        at, half, quarter, part = sizes(s)
        total(s, CORE).wait_recv()

        def body(i):
            rows = ds(own_half(s) + i * 128, 128)
            got = pl.ds(pl.multiple_of(at // 2 + i * 128, 128), 128)
            summed = g_v[rows, :] + rbc[got, :].astype(F32)
            g_v[rows, :] = summed
            sby[got, :] = summed.astype(BF)

        loop(half // 128, body)
        if s == 0:
            each(NY, lambda d: send(
                s, Y, sby.at[ds(at // 2 + part_at(s, lax.rem(y + d, NY), 0), quarter)],
                rby.at[ds(at // 8 * 3 + (d - 1) * quarter, quarter)], y_peer(d),
            ))
        else:
            def blocks(i):
                d, tz = 1 + lax.div(i, NZ), lax.rem(i, NZ)
                send(
                    s, Y, sby.at[ds(at // 2 + part_at(s, lax.rem(y + d, NY), tz), part)],
                    rby.at[ds(at // 8 * 3 + (d - 1) * quarter + tz * part, part)], y_peer(d),
                )

            loop((NY - 1) * NZ, blocks)

    def z_send(s):
        at, half, quarter, part = sizes(s)
        total(s, Y).wait_recv()

        def body(i):
            rows = ds(own_half(s) + part_at(s, y, i), part)
            summed = g_v[rows, :]
            for d in range(NY - 1):
                summed = summed + rby[ds(at // 8 * 3 + d * quarter + i * part, part), :].astype(F32)
            g_v[rows, :] = summed
            sbz[ds(at // 8 + i * part, part), :] = summed.astype(BF)

        loop(NZ, body)
        each(NZ, lambda d: send(
            s, Z, sbz.at[ds(at // 8 + lax.rem(z + d, NZ) * part, part)],
            rbz.at[ds(at // 64 * 7 + (d - 1) * part, part)], z_peer(d),
        ))

    def x_send(s):
        at, half, quarter, part = sizes(s)
        total(s, Z).wait_recv()
        summed = g_v[ds(own_half(s) + part_at(s, y, z), part), :]
        for d in range(NZ - 1):
            summed = summed + rbz[ds(at // 64 * 7 + d * part, part), :].astype(F32)
        rows = ds(at // 64 * 4 + x * part, part)
        sbx[pl.ds(at // 64, part), :] = summed.astype(BF)
        rbx[rows, :] = summed.astype(BF)
        each(NX, lambda d: send(s, X, sbx.at[pl.ds(at // 64, part)], rbx.at[rows], x_peer(d)))

    def summed_over_x(s):
        at, half, quarter, part = sizes(s)
        total(s, X).wait_recv()
        summed = rbx[pl.ds(at // 64 * 4, part), :].astype(F32)
        for k in range(1, NX):
            summed = summed + rbx[pl.ds(at // 64 * 4 + k * part, part), :].astype(F32)
        rows = ds(own_half(s) + part_at(s, y, z), part)
        gg_v[rows, :] = summed.astype(BF)
        return gg_v.at[rows]

    def gather(s):
        ref = summed_over_x(s)
        if s == 0:
            each(NZ, lambda d: send(s, GZ, ref, ref, z_peer(d)))
        else:
            each(NY, lambda d: send(s, GY, ref, ref, y_peer(d)))

    def gather_more(s):
        at, half, quarter, part = sizes(s)
        if s == 0:
            total(s, GZ).wait_recv()
            ref = gg_v.at[ds(own_half(s) + part_at(s, y, 0), quarter)]
            each(NY, lambda d: send(s, GY, ref, ref, y_peer(d)))
        else:
            total(s, GY).wait_recv()
            ref = gg_v.at[ds(own_half(s) + part_at(s, 0, z), NY * part)]
            each(NZ, lambda d: send(s, GZ, ref, ref, z_peer(d)))

    def late_rows(s):
        return ds(own_half(s) + xy_at(0) * SHARE, SHARE)

    def xy_send(s):
        at, half, *_ = sizes(s)
        k = s - LATE
        total(s, CORE).wait_recv()

        def body(i):
            rows = ds(own_half(s) + i * SHARE, SHARE)
            summed = g_v[rows, :] + rbc[ds(at // 2 + i * SHARE, SHARE), :].astype(F32)
            g_v[rows, :] = summed
            late_s[k, i] = summed.astype(BF)

        loop(NP, body)
        each(NP, lambda d: send(s, Y, late_s.at[k, xy_at(d)], late_r.at[k, d - 1], xy_peer(d)))

    def z_all(s):
        k = s - LATE
        total(s, Y).wait_recv()
        summed = g_v[late_rows(s), :]
        for d in range(NP - 1):
            summed = summed + late_r[k, d].astype(F32)
        late_zs[k] = summed.astype(BF)
        late_z[k, z] = summed.astype(BF)
        each(NZ, lambda d: send(s, Z, late_zs.at[k], late_z.at[k, z], z_peer(d)))

    def xy_gather(s):
        k = s - LATE
        total(s, Z).wait_recv()
        summed = late_z[k, 0].astype(F32)
        for i in range(1, NZ):
            summed = summed + late_z[k, i].astype(F32)
        gg_v[late_rows(s), :] = summed.astype(BF)
        ref = gg_v.at[late_rows(s)]
        each(NP, lambda d: send(s, GY, ref, ref, xy_peer(d)))

    def core_gather(s):
        total(s, GZ if s == 1 else GY).wait_recv()
        ref = gg_v.at[ds(own_half(s), sizes(s)[1])]
        send(s, GC, ref, ref, sibling)

    def finish(s):
        total(s, GC).wait_recv()

    vec_stages = ((vc, 2, core, lambda d: sibling), (vy, NY, y, y_peer), (vz, NZ, z, z_peer), (vx, NX, x, x_peer))

    def vec_all(stage):
        ref, n, _, _ = vec_stages[stage]
        whole = ref.at[pl.ds(0, n - 1)]
        return pltpu.make_async_remote_copy(
            src_ref=whole, dst_ref=whole, send_sem=vec_send.at[stage], recv_sem=vec_recv.at[stage],
            device_id=sibling, device_id_type=MESH,
        )

    def vec_step(stage):
        if stage == 0:
            value = vs[0]
        else:
            vec_all(stage - 1).wait_recv()
            before, n, _, _ = vec_stages[stage - 1]
            value = before[0]
            for k in range(1, n):
                value = value + before[k]
        if stage == len(vec_stages):
            vec_ref[...] = value
            return
        ref, n, me, peer = vec_stages[stage]
        vs[stage] = value
        ref[me] = value

        def to(d, carry):
            pltpu.make_async_remote_copy(
                src_ref=vs.at[stage], dst_ref=ref.at[me],
                send_sem=vec_send.at[stage], recv_sem=vec_recv.at[stage],
                device_id=peer(d), device_id_type=MESH,
            ).start()
            return carry

        lax.fori_loop(1, n, to, 0)

    def transpose(r):
        for r in range(NB):
            rows = pl.ds(r * 256, 256)
            actt_v[:, rows] = act_v[rows, :].T

    def kg1_and_mixer(c, n):
        lanes = slice(c * W, (c + n) * W)
        for r in range(NB):
            rows = pl.ds(r * 256, 256)
            hidt_v[lanes, rows] = hid_v[rows, lanes].T

        def kg1(m):
            part = nn(actt_v[pl.ds(pl.multiple_of(m * 256, 256), 256), :], pg_v[:, lanes])
            for k in range(n):
                at = KG1_AT + (c + k) * PAIR + m * 256
                g_v[pl.ds(pl.multiple_of(at, 256), 256), :] = part[:, k * W:(k + 1) * W]

        loop(C // 256, kg1)
        for j in range(C // 256):
            part = nn(hidt_v[lanes, :], cot_v[:, j * 256:(j + 1) * 256])
            for i in range(n):
                for k in range(2):
                    at = MG_AT + (c + i) * PAIR + (j * 2 + k) * W
                    g_v[pl.ds(at, W), :] = part[i * W:(i + 1) * W, k * W:(k + 1) * W]

    def vectors():
        ones = jnp.ones((8, ROWS), BF)
        cot_sum = nn(ones, cot_v[...])
        pg_sum = nn(ones, pg_v[...])
        for j in range(C // W):
            vs[0, j:j + 1, :] = cot_sum[:1, j * W:(j + 1) * W]
        for j in range(H // W):
            vs[0, C // W + j:C // W + j + 1, :] = pg_sum[:1, j * W:(j + 1) * W]
        done = C // W + H // W
        vs[0, done:, :] = jnp.zeros((VEC - done, W), F32)

    def kg02(c):
        def wait(r):
            for copy in pg_copies(c, r):
                copy.wait_recv()

        loop(NR, wait)

        def block(m):
            part = nn(actt_v[pl.ds(pl.multiple_of(m * 256, 256), 256), :], pg02_v[c])
            early, late = part[:, :W], part[:, W:]
            if c == 0:
                at = KG02_AT + m * 256
                g_v[pl.ds(pl.multiple_of(at, 256), 256), :] = early
                g_v[pl.ds(pl.multiple_of(at + C, 256), 256), :] = late
            else:
                s = LATE + c - 1
                g_v[pl.ds(pl.multiple_of(own_half(s) + m * 256, 256), 256), :] = jnp.where(core == 0, early, late)
                sbc[pl.ds(pl.multiple_of(SEGS[s][0] // 2 + m * 256, 256), 256), :] = jnp.where(
                    core == 0, late, early
                ).astype(BF)

        loop(C // 256, block)

    def leave(r):
        rows = pl.ds(pl.multiple_of(r * 256, 256), 256)
        lo_v[rows, :] = (f_v[rows, :].astype(F32) + nn(hid_v[rows, :], mix_v[...]) + bias_v[...].reshape(1, C)).astype(BF)

    def grad_part(r):
        rows = pl.ds(pl.multiple_of(r * 256, 256), 256)
        grad_v[rows, :] = nt(pg_v[rows, :], k1_v[...]) + nt(pg02_v[0, rows, :], kw_v[0])

    def grad_in(r):
        rows = pl.ds(pl.multiple_of(r * 256, 256), 256)
        grad = grad_v[rows, :]
        for c in range(1, NC):
            grad = grad + nt(pg02_v[c, rows, :], kw_v[c])
        ig_v[rows, :] = (cot_v[rows, :].astype(F32) + grad * slope_v[rows, :]).astype(BF)

    hidden(0)
    transpose(0)
    hidden(1)
    kg1_and_mixer(0, 2)
    core_send(0)
    hidden(2, 0, NR // 2)
    y_send(0)
    hidden(2, NR // 2, NR)
    kg1_and_mixer(2, 1)
    vectors()
    vec_step(0)
    loop(NB, leave)
    z_send(0)
    vec_step(1)
    kg02(0)
    core_send(1)
    vec_step(2)
    y_send(1)
    loop(NB, grad_part)
    kg02(1)
    core_send(2)
    z_send(1)
    xy_send(2)
    kg02(2)
    core_send(3)
    x_send(0)
    xy_send(3)
    x_send(1)
    vec_step(3)
    gather(0)
    z_all(2)
    gather(1)
    z_all(3)
    grad_in(0)
    gather_more(1)
    gather_more(0)
    grad_in(1)
    xy_gather(2)
    xy_gather(3)
    grad_in(2)
    grad_in(3)
    vec_step(4)
    core_gather(2)
    core_gather(0)
    core_gather(1)
    core_gather(3)
    for s in range(len(SEGS)):
        finish(s)

    for d, ref in ((0, t0_v), (1, t2_v), (2, t0_v), (3, t2_v)):
        pltpu.make_async_remote_copy(
            src_ref=ref, dst_ref=ref, send_sem=halo_send.at[d], recv_sem=tap_recv.at[0, 0, 0],
            device_id=sibling, device_id_type=MESH,
        ).wait_send()
    for stage in range(len(vec_stages)):
        vec_all(stage).wait_send()
    for s in range(len(SEGS)):
        for stage in range(7):
            if s < LATE or stage not in (X, GZ):
                total(s, stage).wait_send()


def finish_kernel(
    factor, lo_v, ig_v, gg_v, vec_in, lo_out, ig_out, kg_out, mg_out, offset_out, biases_out, kg_v, mg_v, sem
):
    stores = [
        pltpu.make_async_copy(lo_v, lo_out, sem.at[0]),
        pltpu.make_async_copy(ig_v, ig_out, sem.at[1]),
        pltpu.make_async_copy(mg_v, mg_out, sem.at[2]),
    ]
    stores += [pltpu.make_async_copy(kg_v.at[k], kg_out.at[k], sem.at[3 + k]) for k in range(3)]

    for copy in stores[:2]:
        copy.start()

    def spread(k, start):
        for c in range(NC):
            def body(i, carry, c=c):
                rows = pl.ds(pl.multiple_of(i * 128, 128), 128)
                source = pl.ds(pl.multiple_of(start + c * PAIR + i * 128, 128), 128)
                kg_v[k, rows, c * W:(c + 1) * W] = gg_v[source, :].astype(F32) * factor
                return carry

            lax.fori_loop(0, C // 128, body, 0)
        stores[3 + k].start()

    spread(1, KG1_AT)
    spread(0, KG02_AT)
    spread(2, KG02_AT + C)
    for c in range(H // W):
        for j in range(C // W):
            at = MG_AT + c * PAIR + j * W
            mg_v[c * W:(c + 1) * W, j * W:(j + 1) * W] = gg_v[at:at + W, :].astype(F32) * factor
    stores[2].start()
    vec = vec_in[...] * factor
    biases_out[...] = vec[:C // W].reshape(C)
    offset_out[...] = vec[C // W:(C + H) // W].reshape(H)
    for copy in stores:
        copy.wait()


def local(features, kernel, offsets, mixer, biases, cotangent):
    length = features.shape[0] * lax.axis_size("seq") * lax.axis_size("sub")
    factor = 1.0 / math.sqrt(length)
    hbm_spec = pl.BlockSpec(memory_space=pltpu.HBM)
    vmem_spec = pl.BlockSpec(memory_space=pltpu.VMEM)
    n = len(SEGS)
    vm = pltpu.VMEM
    dma = pltpu.SemaphoreType.DMA
    lo, ig, gg, vec = pl.pallas_call(
        main_kernel,
        out_shape=(
            jax.ShapeDtypeStruct((ROWS, C), BF),
            jax.ShapeDtypeStruct((ROWS, C), BF),
            jax.ShapeDtypeStruct((TOTAL, W), BF),
            jax.ShapeDtypeStruct((VEC, W), F32),
        ),
        in_specs=[hbm_spec] * 6,
        out_specs=(vmem_spec,) * 4,
        scratch_shapes=[
            vm((ROWS, C), BF), vm((ROWS, C), BF), vm((NC, C, 2 * W), BF), vm((C, H), BF), vm((H, C), BF), vm((H,), F32), vm((C,), F32),
            vm((ROWS, C), BF), vm((C, ROWS), BF), vm((ROWS, C), F32), vm((ROWS, C), F32), vm((ROWS, H), F32), vm((ROWS, H), F32),
            vm((NC, ROWS, W), BF), vm((NC, ROWS, W), BF), vm((NC, ROWS, W), BF), vm((NC, ROWS, W), BF),
            vm((ROWS, H), BF), vm((H, ROWS), BF), vm((ROWS, H), BF), vm((NC, ROWS, 2 * W), BF),
            vm((TOTAL, W), F32),
            vm((TOTAL // 2, W), BF), vm((TOTAL // 2, W), BF), vm((TOTAL // 2, W), BF), vm((TOTAL // 8 * 3, W), BF),
            vm((TOTAL // 8, W), BF), vm((TOTAL // 64 * 7, W), BF), vm((TOTAL // 64, W), BF),
            vm((TOTAL // 64 * 4, W), BF),
            vm((2, NP, SHARE, W), BF), vm((2, NP - 1, SHARE, W), BF), vm((2, SHARE, W), BF), vm((2, NZ, SHARE, W), BF),
            vm((4, VEC, W), F32), vm((2, VEC, W), F32), vm((NY, VEC, W), F32), vm((NZ, VEC, W), F32),
            vm((NX, VEC, W), F32),
            dma((NR,)), dma((2 * NC + 5,)), dma((4,)), dma((2, NC, NR)), dma((2, NC, NR)),
            dma((n, 7)), dma((n, 7)), dma((4,)), dma((4,)),
        ],
        compiler_params=pltpu.CompilerParams(
            collective_id=0, has_side_effects=True, vmem_limit_bytes=46 * 2**20
        ),
        cost_estimate=pl.CostEstimate(flops=8_000_000_000, bytes_accessed=16_000_000, transcendentals=1_200_000),
        name="block",
    )(*[pltpu.with_memory_space_constraint(v, pltpu.HBM) for v in (features, kernel, offsets, mixer, biases, cotangent)])
    layer_output, input_grad, kernel_grad, mixer_grad, offset_grad, biases_grad = pl.pallas_call(
        lambda *refs: finish_kernel(factor, *refs),
        out_shape=(
            jax.ShapeDtypeStruct((ROWS, C), BF),
            jax.ShapeDtypeStruct((ROWS, C), BF),
            jax.ShapeDtypeStruct((3, C, H), F32),
            jax.ShapeDtypeStruct((H, C), F32),
            jax.ShapeDtypeStruct((H,), F32),
            jax.ShapeDtypeStruct((C,), F32),
        ),
        in_specs=[vmem_spec] * 4,
        out_specs=(hbm_spec,) * 4 + (vmem_spec,) * 2,
        scratch_shapes=[vm((3, C, H), F32), vm((H, C), F32), dma((6,))],
        compiler_params=pltpu.CompilerParams(vmem_limit_bytes=12 * 2**20),
        name="finish",
    )(lo, ig, gg, vec)
    return (layer_output, input_grad, kernel_grad, offset_grad, mixer_grad, biases_grad)


def solution(mesh):
    placed = (P(("seq", "sub"), None), P(), P(), P(), P(), P(("seq", "sub"), None))
    return jax.shard_map(
        local,
        mesh=mesh,
        in_specs=placed,
        out_specs=(P(("seq", "sub"), None), P(("seq", "sub"), None), P(), P(), P(), P()),
        check_vma=False,
    )
```

```python
import math

import jax
import jax.numpy as jnp
from jax import lax
from jax.experimental import pallas as pl
from jax.experimental.pallas import tpu as pltpu
from jax.sharding import PartitionSpec as P

MESH = pl.DeviceIdType.MESH
BF = jnp.bfloat16
F32 = jnp.float32

DILATION_STEP = 8192
C = 768
H = 384
ROWS = 1024
W = 128
NC = H // W
NR = 4
RB = ROWS // NR
NB = ROWS // 256

NX, NY, NZ = 4, 4, 8

PAIR = 2 * C
KG1_AT, MG_AT, KG02_AT = 0, C, NC * PAIR
TOTAL = 2 * NC * PAIR
SEGS = ((0, 3072), (3072, 3072), (6144, 1536), (7680, 1536))
LATE = 2
NP = NX * NY
SHARE = SEGS[LATE][1] // (2 * NP)
VEC = 16

T_SCALE = 0.3
TAIL = (
    0.11962923731872051,
    0.12075488221323095,
    0.0999078411835699,
    0.12857978094297895,
    -0.05371691656802647,
    0.20638841535029362,
    -0.1572225638776185,
    0.03567924927328374,
)


def gelu_and_slope(v):
    u = jnp.abs(v)
    t = 1.0 / (1.0 + T_SCALE * u)
    poly = TAIL[-1]
    for coef in TAIL[-2::-1]:
        poly = poly * t + coef
    bell = jnp.exp(-0.5 * u * u)
    tail = poly * t * bell
    cdf = jnp.where(v >= 0.0, 1.0 - tail, tail)
    return v * cdf, cdf + v * bell * (1.0 / math.sqrt(2.0 * math.pi))


def nn(a, b):
    return jnp.dot(a, b, preferred_element_type=F32)


def nt(a, b):
    return lax.dot_general(a, b, (((1,), (1,)), ((), ())), preferred_element_type=F32)


def position():
    seq, sub = lax.axis_index("seq"), lax.axis_index("sub")
    z, x = lax.div(seq, 2 * NX), lax.rem(lax.div(seq, 2), NX)
    y = lax.div(sub, 2) * 2 + lax.rem(seq, 2)
    return seq, sub, x, y, z, lax.rem(sub, 2)


def device(x, y, z, core):
    return (z * (2 * NX) + x * 2 + lax.rem(y, 2), lax.div(y, 2) * 2 + core)


def main_kernel(
    f_hbm, k_hbm, off_hbm, mix_hbm, bias_hbm, cot_hbm,
    lo_v, ig_v, gg_v, vec_ref,
    f_v, cot_v, kw_v, k1_v, mix_v, off_v, bias_v,
    act_v, actt_v, slope_v, grad_v, pre_v, hg_v,
    t0_v, t2_v, te_v, tl_v, hid_v, hidt_v, pg_v, pg02_v,
    g_v, sbc, rbc, sby, rby, sbz, rbz, sbx, rbx,
    late_s, late_r, late_zs, late_z,
    vs, vc, vy, vz, vx,
    f_sem, in_sem, halo_send, tap_recv, pg_recv, seg_send, seg_recv, vec_send, vec_recv,
):
    seq, sub, x, y, z, core = position()
    nseq = 2 * NX * NZ
    ahead = (lax.rem(seq + 2, nseq), sub)
    behind = (lax.rem(seq + nseq - 2, nseq), sub)

    def y_peer(d):
        return device(x, lax.rem(y + d, NY), z, core)

    def z_peer(d):
        return device(x, y, lax.rem(z + d, NZ), core)

    def x_peer(d):
        return device(lax.rem(x + d, NX), y, z, core)

    def xy_at(d):
        return lax.rem(x * NY + y + d, NP)

    def xy_peer(d):
        return device(lax.div(xy_at(d), NY), lax.rem(xy_at(d), NY), z, core)

    sibling = device(x, y, z, 1 - core)

    barrier = pltpu.get_barrier_semaphore()

    def greet(to):
        pl.semaphore_signal(barrier, inc=1, device_id=to, device_id_type=MESH)

    def greet_loop(n, peer):
        def body(d, carry):
            greet(peer(d))
            return carry

        lax.fori_loop(1, n, body, 0)

    def f_copy(r):
        rows = pl.ds(pl.multiple_of(r * RB, RB), RB)
        return pltpu.make_async_copy(f_hbm.at[rows], f_v.at[rows], f_sem.at[r])

    ins = []
    for c in range(NC):
        lanes = pl.ds(c * W, W)
        ins.append((k_hbm.at[0, :, lanes], kw_v.at[c, :, pl.ds(0, W)]))
        ins.append((k_hbm.at[2, :, lanes], kw_v.at[c, :, pl.ds(W, W)]))
    ins.append((k_hbm.at[1], k1_v))
    ins.append((mix_hbm, mix_v))
    ins.append((cot_hbm, cot_v))
    ins.append((off_hbm, off_v))
    ins.append((bias_hbm, bias_v))
    ins = [pltpu.make_async_copy(s, d, in_sem.at[i]) for i, (s, d) in enumerate(ins)]
    f_copy(0).start()
    ins[0].start()
    ins[1].start()
    for r in range(1, 3):
        f_copy(r).start()
    ins[2].start()
    ins[3].start()
    for r in range(3, NR):
        f_copy(r).start()
    for copy in ins[4:]:
        copy.start()

    greet(sibling)
    greet(ahead)
    greet(behind)
    greet_loop(NP, xy_peer)
    greet_loop(NZ, z_peer)

    def loop(n, body):
        def step(i, carry):
            body(i)
            return carry

        lax.fori_loop(0, n, step, 0)

    def rows_at(base, i, n):
        return pl.ds(pl.multiple_of(base + i * n, n), n)

    def activate(r):
        def body(i):
            rows = pl.ds(pl.multiple_of(r * RB + i * 16, 16), 16)
            gelu, slope = gelu_and_slope(f_v[rows, :].astype(F32))
            act_v[rows, :] = gelu.astype(BF)
            slope_v[rows, :] = slope

        loop(RB // 16, body)

    def tap_copies(c, r):
        rows = pl.ds(pl.multiple_of(r * RB, RB), RB)
        return (
            pltpu.make_async_remote_copy(
                src_ref=t0_v.at[c, rows], dst_ref=te_v.at[c, rows],
                send_sem=halo_send.at[0], recv_sem=tap_recv.at[0, c, r],
                device_id=ahead, device_id_type=MESH,
            ),
            pltpu.make_async_remote_copy(
                src_ref=t2_v.at[c, rows], dst_ref=tl_v.at[c, rows],
                send_sem=halo_send.at[1], recv_sem=tap_recv.at[1, c, r],
                device_id=behind, device_id_type=MESH,
            ),
        )

    def taps(c, r):
        rows = pl.ds(pl.multiple_of(r * RB, RB), RB)
        both = nn(act_v[rows, :], kw_v[c]).astype(BF)
        t0_v[c, rows, :] = both[:, :W]
        t2_v[c, rows, :] = both[:, W:]

    def send_taps(c, r):
        for copy in tap_copies(c, r):
            copy.start()

    def taps_of_two(r):
        for c in range(2):
            taps(c, r)
        for c in range(2):
            send_taps(c, r)

    f_copy(0).wait()
    activate(0)
    for copy in ins[:4]:
        copy.wait()
    taps(0, 0)
    pl.semaphore_wait(barrier, 1 + 2 + (NP - 1) + (NZ - 1))
    send_taps(0, 0)
    taps(1, 0)
    send_taps(1, 0)

    def first(i):
        r = i + 1
        f_copy(r).wait()
        activate(r)
        taps_of_two(r)

    loop(NR - 1, first)
    for copy in ins[4:6]:
        copy.wait()

    def third(r):
        taps(2, r)
        send_taps(2, r)

    loop(NR, third)
    for copy in ins[2 * NC:]:
        copy.wait()

    def own(r):
        rows = pl.ds(pl.multiple_of(r * 256, 256), 256)
        pre_v[rows, :] = nn(act_v[rows, :], k1_v[...]) + off_v[...].reshape(1, H)
        hg_v[rows, :] = nt(cot_v[rows, :], mix_v[...])

    with jax.named_scope("own"):
        loop(NB, own)

    def pg_copies(c, r):
        rows = pl.ds(pl.multiple_of(r * RB, RB), RB)
        src = pg_v.at[rows, pl.ds(c * W, W)]
        return (
            pltpu.make_async_remote_copy(
                src_ref=src, dst_ref=pg02_v.at[c, rows, pl.ds(0, W)],
                send_sem=halo_send.at[2], recv_sem=pg_recv.at[0, c, r],
                device_id=behind, device_id_type=MESH,
            ),
            pltpu.make_async_remote_copy(
                src_ref=src, dst_ref=pg02_v.at[c, rows, pl.ds(W, W)],
                send_sem=halo_send.at[3], recv_sem=pg_recv.at[1, c, r],
                device_id=ahead, device_id_type=MESH,
            ),
        )

    def hidden(c, first=0, last=NR):
        lanes = slice(c * W, (c + 1) * W)

        def block(r):
            for copy in tap_copies(c, r):
                copy.wait_recv()

            def body(i):
                rows = pl.ds(pl.multiple_of(r * RB + i * 64, 64), 64)
                pre = pre_v[rows, lanes] + te_v[c, rows, :].astype(F32) + tl_v[c, rows, :].astype(F32)
                gelu, slope = gelu_and_slope(pre)
                hid_v[rows, lanes] = gelu.astype(BF)
                pg_v[rows, lanes] = (hg_v[rows, lanes] * slope).astype(BF)

            loop(RB // 64, body)
            for copy in pg_copies(c, r):
                copy.start()

        loop(last - first, lambda i: block(first + i))

    CORE, Y, Z, X, GZ, GY, GC = range(7)

    def ds(base, n):
        return pl.ds(pl.multiple_of(base, 16), n)

    def sizes(s):
        at, n = SEGS[s]
        return at, n // 2, n // 8, n // 64

    def own_half(s):
        at, half, *_ = sizes(s)
        return at + core * half

    def part_at(s, ty, tz):
        return (ty * NZ + tz if s == 0 else tz * NY + ty) * sizes(s)[3]

    def send(s, stage, src, dst, to):
        pltpu.make_async_remote_copy(
            src_ref=src, dst_ref=dst, send_sem=seg_send.at[s, stage], recv_sem=seg_recv.at[s, stage],
            device_id=to, device_id_type=MESH,
        ).start()

    def each(n, body):
        def step(d, carry):
            body(d)
            return carry

        lax.fori_loop(1, n, step, 0)

    def bulk(s, stage):
        at, half, quarter, part = sizes(s)
        if stage in (CORE, GC):
            return rbc.at[pl.ds(at // 2, half)]
        if s >= LATE:
            return late_z.at[s - LATE, pl.ds(0, NZ - 1)] if stage == Z else late_r.at[s - LATE]
        if s == 1 and stage == GY:
            return rbc.at[pl.ds(at // 2, (NY - 1) * part)]
        if s == 1 and stage == GZ:
            return rbc.at[pl.ds(at // 2, (NZ - 1) * NY * part)]
        if stage in (Y, GY):
            return rby.at[pl.ds(at // 8 * 3, 3 * quarter)]
        if stage in (Z, GZ):
            return rbz.at[pl.ds(at // 64 * 7, 7 * part)]
        return rbx.at[pl.ds(at // 64 * 4, 3 * part)]

    def total(s, stage):
        ref = bulk(s, stage)
        return pltpu.make_async_remote_copy(
            src_ref=ref, dst_ref=ref, send_sem=seg_send.at[s, stage], recv_sem=seg_recv.at[s, stage],
            device_id=sibling, device_id_type=MESH,
        )

    def core_send(s):
        at, half, *_ = sizes(s)
        other = at + (1 - core) * half

        def body(i):
            sbc[pl.ds(pl.multiple_of(at // 2 + i * 128, 128), 128), :] = g_v[
                ds(other + i * 128, 128), :
            ].astype(BF)

        if s < LATE:
            loop(half // 128, body)
        rows = pl.ds(at // 2, half)
        send(s, CORE, sbc.at[rows], rbc.at[rows], sibling)

    def y_send(s):
        at, half, quarter, part = sizes(s)
        total(s, CORE).wait_recv()

        def body(i):
            rows = ds(own_half(s) + i * 128, 128)
            got = pl.ds(pl.multiple_of(at // 2 + i * 128, 128), 128)
            summed = g_v[rows, :] + rbc[got, :].astype(F32)
            g_v[rows, :] = summed
            sby[got, :] = summed.astype(BF)

        loop(half // 128, body)
        if s == 0:
            each(NY, lambda d: send(
                s, Y, sby.at[ds(at // 2 + part_at(s, lax.rem(y + d, NY), 0), quarter)],
                rby.at[ds(at // 8 * 3 + (d - 1) * quarter, quarter)], y_peer(d),
            ))
        else:
            def blocks(i):
                d, tz = 1 + lax.div(i, NZ), lax.rem(i, NZ)
                send(
                    s, Y, sby.at[ds(at // 2 + part_at(s, lax.rem(y + d, NY), tz), part)],
                    rby.at[ds(at // 8 * 3 + (d - 1) * quarter + tz * part, part)], y_peer(d),
                )

            loop((NY - 1) * NZ, blocks)

    def z_send(s):
        at, half, quarter, part = sizes(s)
        total(s, Y).wait_recv()

        def body(i):
            rows = ds(own_half(s) + part_at(s, y, i), part)
            summed = g_v[rows, :]
            for d in range(NY - 1):
                summed = summed + rby[ds(at // 8 * 3 + d * quarter + i * part, part), :].astype(F32)
            g_v[rows, :] = summed
            sbz[ds(at // 8 + i * part, part), :] = summed.astype(BF)

        loop(NZ, body)
        each(NZ, lambda d: send(
            s, Z, sbz.at[ds(at // 8 + lax.rem(z + d, NZ) * part, part)],
            rbz.at[ds(at // 64 * 7 + (d - 1) * part, part)], z_peer(d),
        ))

    def x_send(s):
        at, half, quarter, part = sizes(s)
        total(s, Z).wait_recv()
        summed = g_v[ds(own_half(s) + part_at(s, y, z), part), :]
        for d in range(NZ - 1):
            summed = summed + rbz[ds(at // 64 * 7 + d * part, part), :].astype(F32)
        rows = ds(at // 64 * 4 + x * part, part)
        sbx[pl.ds(at // 64, part), :] = summed.astype(BF)
        rbx[rows, :] = summed.astype(BF)
        each(NX, lambda d: send(s, X, sbx.at[pl.ds(at // 64, part)], rbx.at[rows], x_peer(d)))

    def summed_over_x(s):
        at, half, quarter, part = sizes(s)
        total(s, X).wait_recv()
        summed = rbx[pl.ds(at // 64 * 4, part), :].astype(F32)
        for k in range(1, NX):
            summed = summed + rbx[pl.ds(at // 64 * 4 + k * part, part), :].astype(F32)
        rows = ds(own_half(s) + part_at(s, y, z), part)
        gg_v[rows, :] = summed.astype(BF)
        return gg_v.at[rows]

    def gather(s):
        ref = summed_over_x(s)
        if s == 0:
            each(NZ, lambda d: send(s, GZ, ref, ref, z_peer(d)))
        else:
            each(NY, lambda d: send(s, GY, ref, ref, y_peer(d)))

    def gather_more(s):
        at, half, quarter, part = sizes(s)
        if s == 0:
            total(s, GZ).wait_recv()
            ref = gg_v.at[ds(own_half(s) + part_at(s, y, 0), quarter)]
            each(NY, lambda d: send(s, GY, ref, ref, y_peer(d)))
        else:
            total(s, GY).wait_recv()
            ref = gg_v.at[ds(own_half(s) + part_at(s, 0, z), NY * part)]
            each(NZ, lambda d: send(s, GZ, ref, ref, z_peer(d)))

    def late_rows(s):
        return ds(own_half(s) + xy_at(0) * SHARE, SHARE)

    def xy_send(s):
        at, half, *_ = sizes(s)
        k = s - LATE
        total(s, CORE).wait_recv()

        def body(i):
            rows = ds(own_half(s) + i * SHARE, SHARE)
            summed = g_v[rows, :] + rbc[ds(at // 2 + i * SHARE, SHARE), :].astype(F32)
            g_v[rows, :] = summed
            late_s[k, i] = summed.astype(BF)

        loop(NP, body)
        each(NP, lambda d: send(s, Y, late_s.at[k, xy_at(d)], late_r.at[k, d - 1], xy_peer(d)))

    def z_all(s):
        k = s - LATE
        total(s, Y).wait_recv()
        summed = g_v[late_rows(s), :]
        for d in range(NP - 1):
            summed = summed + late_r[k, d].astype(F32)
        late_zs[k] = summed.astype(BF)
        late_z[k, z] = summed.astype(BF)
        each(NZ, lambda d: send(s, Z, late_zs.at[k], late_z.at[k, z], z_peer(d)))

    def xy_gather(s):
        k = s - LATE
        total(s, Z).wait_recv()
        summed = late_z[k, 0].astype(F32)
        for i in range(1, NZ):
            summed = summed + late_z[k, i].astype(F32)
        gg_v[late_rows(s), :] = summed.astype(BF)
        ref = gg_v.at[late_rows(s)]
        each(NP, lambda d: send(s, GY, ref, ref, xy_peer(d)))

    def core_gather(s):
        total(s, GZ if s == 1 else GY).wait_recv()
        ref = gg_v.at[ds(own_half(s), sizes(s)[1])]
        send(s, GC, ref, ref, sibling)

    def finish(s):
        total(s, GC).wait_recv()

    vec_stages = ((vc, 2, core, lambda d: sibling), (vy, NY, y, y_peer), (vz, NZ, z, z_peer), (vx, NX, x, x_peer))

    def vec_all(stage):
        ref, n, _, _ = vec_stages[stage]
        whole = ref.at[pl.ds(0, n - 1)]
        return pltpu.make_async_remote_copy(
            src_ref=whole, dst_ref=whole, send_sem=vec_send.at[stage], recv_sem=vec_recv.at[stage],
            device_id=sibling, device_id_type=MESH,
        )

    def vec_step(stage):
        if stage == 0:
            value = vs[0]
        else:
            vec_all(stage - 1).wait_recv()
            before, n, _, _ = vec_stages[stage - 1]
            value = before[0]
            for k in range(1, n):
                value = value + before[k]
        if stage == len(vec_stages):
            vec_ref[...] = value
            return
        ref, n, me, peer = vec_stages[stage]
        vs[stage] = value
        ref[me] = value

        def to(d, carry):
            pltpu.make_async_remote_copy(
                src_ref=vs.at[stage], dst_ref=ref.at[me],
                send_sem=vec_send.at[stage], recv_sem=vec_recv.at[stage],
                device_id=peer(d), device_id_type=MESH,
            ).start()
            return carry

        lax.fori_loop(1, n, to, 0)

    def transpose(r):
        for r in range(NB):
            rows = pl.ds(r * 256, 256)
            actt_v[:, rows] = act_v[rows, :].T

    def kg1_and_mixer(c, n):
        lanes = slice(c * W, (c + n) * W)
        for r in range(NB):
            rows = pl.ds(r * 256, 256)
            hidt_v[lanes, rows] = hid_v[rows, lanes].T

        def kg1(m):
            part = nn(actt_v[pl.ds(pl.multiple_of(m * 256, 256), 256), :], pg_v[:, lanes])
            for k in range(n):
                at = KG1_AT + (c + k) * PAIR + m * 256
                g_v[pl.ds(pl.multiple_of(at, 256), 256), :] = part[:, k * W:(k + 1) * W]

        loop(C // 256, kg1)
        for j in range(C // 256):
            part = nn(hidt_v[lanes, :], cot_v[:, j * 256:(j + 1) * 256])
            for i in range(n):
                for k in range(2):
                    at = MG_AT + (c + i) * PAIR + (j * 2 + k) * W
                    g_v[pl.ds(at, W), :] = part[i * W:(i + 1) * W, k * W:(k + 1) * W]

    def vectors():
        ones = jnp.ones((8, ROWS), BF)
        cot_sum = nn(ones, cot_v[...])
        pg_sum = nn(ones, pg_v[...])
        for j in range(C // W):
            vs[0, j:j + 1, :] = cot_sum[:1, j * W:(j + 1) * W]
        for j in range(H // W):
            vs[0, C // W + j:C // W + j + 1, :] = pg_sum[:1, j * W:(j + 1) * W]
        done = C // W + H // W
        vs[0, done:, :] = jnp.zeros((VEC - done, W), F32)

    def kg02(c):
        def wait(r):
            for copy in pg_copies(c, r):
                copy.wait_recv()

        loop(NR, wait)

        def block(m):
            part = nn(actt_v[pl.ds(pl.multiple_of(m * 256, 256), 256), :], pg02_v[c])
            early, late = part[:, :W], part[:, W:]
            if c == 0:
                at = KG02_AT + m * 256
                g_v[pl.ds(pl.multiple_of(at, 256), 256), :] = early
                g_v[pl.ds(pl.multiple_of(at + C, 256), 256), :] = late
            else:
                s = LATE + c - 1
                g_v[pl.ds(pl.multiple_of(own_half(s) + m * 256, 256), 256), :] = jnp.where(core == 0, early, late)
                sbc[pl.ds(pl.multiple_of(SEGS[s][0] // 2 + m * 256, 256), 256), :] = jnp.where(
                    core == 0, late, early
                ).astype(BF)

        loop(C // 256, block)

    def leave(r):
        rows = pl.ds(pl.multiple_of(r * 256, 256), 256)
        lo_v[rows, :] = (f_v[rows, :].astype(F32) + nn(hid_v[rows, :], mix_v[...]) + bias_v[...].reshape(1, C)).astype(BF)

    def grad_part(r):
        rows = pl.ds(pl.multiple_of(r * 256, 256), 256)
        grad_v[rows, :] = nt(pg_v[rows, :], k1_v[...]) + nt(pg02_v[0, rows, :], kw_v[0])

    def grad_in(r):
        rows = pl.ds(pl.multiple_of(r * 256, 256), 256)
        grad = grad_v[rows, :]
        for c in range(1, NC):
            grad = grad + nt(pg02_v[c, rows, :], kw_v[c])
        ig_v[rows, :] = (cot_v[rows, :].astype(F32) + grad * slope_v[rows, :]).astype(BF)

    hidden(0)
    transpose(0)
    hidden(1)
    kg1_and_mixer(0, 2)
    core_send(0)
    hidden(2, 0, NR // 2)
    y_send(0)
    hidden(2, NR // 2, NR)
    kg1_and_mixer(2, 1)
    vectors()
    vec_step(0)
    loop(NB, leave)
    z_send(0)
    vec_step(1)
    kg02(0)
    core_send(1)
    vec_step(2)
    y_send(1)
    loop(NB, grad_part)
    kg02(1)
    core_send(2)
    z_send(1)
    xy_send(2)
    kg02(2)
    core_send(3)
    x_send(0)
    xy_send(3)
    x_send(1)
    vec_step(3)
    gather(0)
    z_all(2)
    gather(1)
    z_all(3)
    grad_in(0)
    gather_more(1)
    gather_more(0)
    grad_in(1)
    xy_gather(2)
    xy_gather(3)
    grad_in(2)
    grad_in(3)
    vec_step(4)
    core_gather(2)
    core_gather(0)
    core_gather(1)
    core_gather(3)
    for s in range(len(SEGS)):
        finish(s)

    for d, ref in ((0, t0_v), (1, t2_v), (2, t0_v), (3, t2_v)):
        pltpu.make_async_remote_copy(
            src_ref=ref, dst_ref=ref, send_sem=halo_send.at[d], recv_sem=tap_recv.at[0, 0, 0],
            device_id=sibling, device_id_type=MESH,
        ).wait_send()
    for stage in range(len(vec_stages)):
        vec_all(stage).wait_send()
    for s in range(len(SEGS)):
        for stage in range(7):
            if s < LATE or stage not in (X, GZ):
                total(s, stage).wait_send()


def finish_kernel(
    factor, lo_v, ig_v, gg_v, vec_in, lo_out, ig_out, kg_out, mg_out, offset_out, biases_out, kg_v, mg_v, sem
):
    stores = [
        pltpu.make_async_copy(lo_v, lo_out, sem.at[0]),
        pltpu.make_async_copy(ig_v, ig_out, sem.at[1]),
        pltpu.make_async_copy(mg_v, mg_out, sem.at[2]),
    ]
    stores += [
        pltpu.make_async_copy(
            kg_v.at[k, pl.ds(part * (C // 2), C // 2)], kg_out.at[k, pl.ds(part * (C // 2), C // 2)],
            sem.at[3 + 2 * k + part],
        )
        for k in range(3)
        for part in range(2)
    ]

    for copy in stores[:2]:
        copy.start()

    def spread(k, start):
        for part in range(2):
            for c in range(NC):
                def body(i, carry, c=c):
                    at = (part * (C // 256) + i) * 128
                    rows = pl.ds(pl.multiple_of(at, 128), 128)
                    source = pl.ds(pl.multiple_of(start + c * PAIR + at, 128), 128)
                    kg_v[k, rows, c * W:(c + 1) * W] = gg_v[source, :].astype(F32) * factor
                    return carry

                lax.fori_loop(0, C // 256, body, 0)
            stores[3 + 2 * k + part].start()

    spread(1, KG1_AT)
    spread(0, KG02_AT)
    spread(2, KG02_AT + C)
    for c in range(H // W):
        for j in range(C // W):
            at = MG_AT + c * PAIR + j * W
            mg_v[c * W:(c + 1) * W, j * W:(j + 1) * W] = gg_v[at:at + W, :].astype(F32) * factor
    stores[2].start()
    vec = vec_in[...] * factor
    biases_out[...] = vec[:C // W].reshape(C)
    offset_out[...] = vec[C // W:(C + H) // W].reshape(H)
    for copy in stores:
        copy.wait()


def local(features, kernel, offsets, mixer, biases, cotangent):
    length = features.shape[0] * lax.axis_size("seq") * lax.axis_size("sub")
    factor = 1.0 / math.sqrt(length)
    hbm_spec = pl.BlockSpec(memory_space=pltpu.HBM)
    vmem_spec = pl.BlockSpec(memory_space=pltpu.VMEM)
    n = len(SEGS)
    vm = pltpu.VMEM
    dma = pltpu.SemaphoreType.DMA
    lo, ig, gg, vec = pl.pallas_call(
        main_kernel,
        out_shape=(
            jax.ShapeDtypeStruct((ROWS, C), BF),
            jax.ShapeDtypeStruct((ROWS, C), BF),
            jax.ShapeDtypeStruct((TOTAL, W), BF),
            jax.ShapeDtypeStruct((VEC, W), F32),
        ),
        in_specs=[hbm_spec] * 6,
        out_specs=(vmem_spec,) * 4,
        scratch_shapes=[
            vm((ROWS, C), BF), vm((ROWS, C), BF), vm((NC, C, 2 * W), BF), vm((C, H), BF), vm((H, C), BF), vm((H,), F32), vm((C,), F32),
            vm((ROWS, C), BF), vm((C, ROWS), BF), vm((ROWS, C), F32), vm((ROWS, C), F32), vm((ROWS, H), F32), vm((ROWS, H), F32),
            vm((NC, ROWS, W), BF), vm((NC, ROWS, W), BF), vm((NC, ROWS, W), BF), vm((NC, ROWS, W), BF),
            vm((ROWS, H), BF), vm((H, ROWS), BF), vm((ROWS, H), BF), vm((NC, ROWS, 2 * W), BF),
            vm((TOTAL, W), F32),
            vm((TOTAL // 2, W), BF), vm((TOTAL // 2, W), BF), vm((TOTAL // 2, W), BF), vm((TOTAL // 8 * 3, W), BF),
            vm((TOTAL // 8, W), BF), vm((TOTAL // 64 * 7, W), BF), vm((TOTAL // 64, W), BF),
            vm((TOTAL // 64 * 4, W), BF),
            vm((2, NP, SHARE, W), BF), vm((2, NP - 1, SHARE, W), BF), vm((2, SHARE, W), BF), vm((2, NZ, SHARE, W), BF),
            vm((4, VEC, W), F32), vm((2, VEC, W), F32), vm((NY, VEC, W), F32), vm((NZ, VEC, W), F32),
            vm((NX, VEC, W), F32),
            dma((NR,)), dma((2 * NC + 5,)), dma((4,)), dma((2, NC, NR)), dma((2, NC, NR)),
            dma((n, 7)), dma((n, 7)), dma((4,)), dma((4,)),
        ],
        compiler_params=pltpu.CompilerParams(
            collective_id=0, has_side_effects=True, vmem_limit_bytes=46 * 2**20
        ),
        cost_estimate=pl.CostEstimate(flops=8_000_000_000, bytes_accessed=16_000_000, transcendentals=1_200_000),
        name="block",
    )(*[pltpu.with_memory_space_constraint(v, pltpu.HBM) for v in (features, kernel, offsets, mixer, biases, cotangent)])
    layer_output, input_grad, kernel_grad, mixer_grad, offset_grad, biases_grad = pl.pallas_call(
        lambda *refs: finish_kernel(factor, *refs),
        out_shape=(
            jax.ShapeDtypeStruct((ROWS, C), BF),
            jax.ShapeDtypeStruct((ROWS, C), BF),
            jax.ShapeDtypeStruct((3, C, H), F32),
            jax.ShapeDtypeStruct((H, C), F32),
            jax.ShapeDtypeStruct((H,), F32),
            jax.ShapeDtypeStruct((C,), F32),
        ),
        in_specs=[vmem_spec] * 4,
        out_specs=(hbm_spec,) * 4 + (vmem_spec,) * 2,
        scratch_shapes=[vm((3, C, H), F32), vm((H, C), F32), dma((9,))],
        compiler_params=pltpu.CompilerParams(vmem_limit_bytes=12 * 2**20),
        name="finish",
    )(lo, ig, gg, vec)
    return (layer_output, input_grad, kernel_grad, offset_grad, mixer_grad, biases_grad)


def solution(mesh):
    placed = (P(("seq", "sub"), None), P(), P(), P(), P(), P(("seq", "sub"), None))
    return jax.shard_map(
        local,
        mesh=mesh,
        in_specs=placed,
        out_specs=(P(("seq", "sub"), None), P(("seq", "sub"), None), P(), P(), P(), P()),
        check_vma=False,
    )
```
